256 devices in a mesh: strip: 64 (over y, x, z_lo, core), lag: 4 (over z_hi).
Axes of the slice: x: 4, y: 4, z: 8 (z_hi: 4, z_lo: 2; z = z_hi * 2 + z_lo), core: 2. Of those that a mesh axis runs over, the one named last changes fastest.
Arguments:
- image_grad: float32 [128, 4096, 1024], P('lag', 'strip'), may hold values from -0.4 to 0.4
- source_field: float32 [2, 4096, 1024], P(None, None, 'strip'), may hold values from -6 to 6
- receiver_field: float32 [2, 4096, 1024], P(None, None, 'strip'), may hold values from -6 to 6
Outputs:
- source_adjoint: float32 [2, 4096, 1024], P(None, 'strip', 'lag')
- receiver_adjoint: float32 [2, 4096, 1024], P(None, 'strip', 'lag')
The draws below stay inside these ranges and needn't reach their ends.
All inputs are finite; a program needn't handle non-finite values.
Results may differ from the reference program's by a relative error of at most 0.0003.
Values sent between devices are 32-bit elements; how exact they have to be, the bound alone decides.
A program may use at most 128 MiB of HBM per device.

```python
import jax
import jax.numpy as jnp
from jax import lax

NX = 1024
NH = 128
SNAP = 2
NZ = 4096


def level_of(rng, extent, shards, low, high):
    def one(axis_at, shards_of):
        steps = jax.random.uniform(jax.random.fold_in(jax.random.fold_in(rng, 6), axis_at), (shards_of,), jnp.float32, low / len(shards), high / len(shards))
        return jnp.repeat(jnp.exp(steps), extent[axis_at] // shards_of).reshape((-1,) + (1,) * (len(extent) - axis_at - 1))

    loudness = one(*shards[0])
    for cut in shards[1:]:
        loudness = loudness * one(*cut)
    return loudness


def bell_draw(rng, shape, scale, bound, split=(), kind=jnp.bfloat16):
    level = level_of(rng, shape, split, -0.22, 0.18) if split else 1.0
    drawn = jax.random.normal(rng, shape, jnp.float32) * scale * level
    return jnp.minimum(jnp.maximum(drawn, -bound), bound).astype(kind)


def setup_inputs(seed: int = 0) -> dict:
    key_list = jax.random.split(jax.random.key(seed), 4)
    image_grad = bell_draw(key_list[0], (NH, NZ, NX), 0.05, 0.4, ((0, 4), (1, 64)), jnp.float32)
    source_field = bell_draw(key_list[1], (SNAP, NZ, NX), 1.0, 6.0, ((2, 64),), jnp.float32)
    receiver_field = bell_draw(key_list[2], (SNAP, NZ, NX), 1.0, 6.0, ((2, 64),), jnp.float32)
    return dict(image_grad=image_grad, source_field=source_field, receiver_field=receiver_field)


def pad_cells(values, width_cells):
    return jnp.pad(values, [(0, 0)] * (values.ndim - 1) + [(width_cells, width_cells)])


def shift_cells(padded_values, offset, width_cells):
    start = (width_cells + offset).astype(jnp.int32)
    return lax.dynamic_slice_in_dim(padded_values, start, width_cells, padded_values.ndim - 1)


def laplace_filter(slab_now):
    padded = jnp.pad(slab_now, 1)
    center = padded[1:-1, 1:-1]
    return 2.0 * center - 0.25 * (padded[2:, 1:-1] + padded[:-2, 1:-1] + padded[1:-1, 2:] + padded[1:-1, :-2])


def reference(image_grad, source_field, receiver_field):
    width_cells = image_grad.shape[2]
    source = pad_cells(source_field, width_cells)
    receiver = pad_cells(receiver_field, width_cells)
    empty_sum = jnp.zeros((source_field.shape[0], image_grad.shape[1], width_cells), jnp.float32)

    def lag_step(totals, lag_number):
        source_total, receiver_total = totals
        slab_now = laplace_filter(lax.dynamic_index_in_dim(image_grad, lag_number, 0, keepdims=False))
        slab_pad = pad_cells(slab_now, width_cells)
        offset = lag_number - NH // 2
        source_total = source_total + shift_cells(slab_pad, offset, width_cells)[None] * shift_cells(receiver, 2 * offset, width_cells)
        receiver_total = receiver_total + shift_cells(slab_pad, -offset, width_cells)[None] * shift_cells(source, -2 * offset, width_cells)
        return (source_total, receiver_total), None

    (source_adjoint, receiver_adjoint), unused = lax.scan(lag_step, (empty_sum, empty_sum), jnp.arange(NH, dtype=jnp.int32))
    return source_adjoint, receiver_adjoint
```

```python
import functools

import jax
import jax.numpy as jnp
from jax import lax
from jax.experimental import pallas as pl
from jax.experimental.pallas import tpu as pltpu
from jax.sharding import PartitionSpec as P

MESH = pl.DeviceIdType.MESH
F32 = jnp.float32

STRIPS = 64
LAGS = 4
NK = 32
ROWS = 64
NX = 1024
XB = NX // 128
COLS = NX // STRIPS
PADX = 128
PADF = 64
SLOT = 80
OUTX = NX // LAGS
SUB = 64
CHUNKS = 8
KC = NK // CHUNKS


def copy_bytes(ref, sem):
    return pltpu.make_async_copy(ref, ref, sem)


def kernel(
    grad, source, receiver, out_s, out_r,
    edge, tiles, filt, packed, raw, field, halo_out, halo_in,
    part, relay, near_in, own,
    edge_sem, raw_sem, load_sem, a2a_send, a2a_recv,
    halo_send, halo_recv, rs_send, rs_recv,
):
    me = lax.axis_index("strip")
    lag = lax.axis_index("lag")
    up_lag = lax.rem(lag + 1, LAGS)
    down_lag = lax.rem(lag + LAGS - 1, LAGS)
    next_strip = lax.rem(me + 1, STRIPS)
    prev_strip = lax.rem(me + STRIPS - 1, STRIPS)

    barrier = pltpu.get_barrier_semaphore()

    def greet(d, carry):
        pl.semaphore_signal(
            barrier, inc=1, device_id=(lax.rem(me + d, STRIPS), lag), device_id_type=MESH
        )
        return carry

    lax.fori_loop(1, STRIPS, greet, 0)
    for other in (up_lag, down_lag):
        pl.semaphore_signal(barrier, inc=1, device_id=(me, other), device_id_type=MESH)

    for b in range(XB):
        lanes = pl.ds(128 * b, 128)
        pltpu.make_async_copy(grad.at[:, 0:8, lanes], edge.at[0, :, b], edge_sem).start()
        pltpu.make_async_copy(
            grad.at[:, ROWS - 8 : ROWS, lanes], edge.at[1, :, b], edge_sem
        ).start()
    pltpu.make_async_copy(source, raw.at[0], raw_sem).start()
    pltpu.make_async_copy(receiver, raw.at[1], raw_sem).start()
    for c in range(CHUNKS):
        for b in range(XB):
            pltpu.make_async_copy(
                grad.at[c * KC : (c + 1) * KC, :, 128 * b : 128 * (b + 1)],
                tiles.at[c * KC : (c + 1) * KC, b, 8 : 8 + ROWS, :],
                load_sem.at[c],
            ).start()

    for f in range(2):
        field[f, 0:PADX, :] = jnp.zeros((PADX, 128), F32)
        field[f, PADX + NX :, :] = jnp.zeros((PADX, 128), F32)
    filt[0:PADF, :] = jnp.zeros((PADF, 128), F32)
    filt[PADF + NK * NX :, :] = jnp.zeros((PADF, 128), F32)

    copy_bytes(edge, edge_sem).wait()
    flat = edge.reshape(2 * NK * XB * 8, 128)
    halo_out[0] = flat[pl.ds(0, NK * XB, stride=8), :]
    halo_out[1] = flat[pl.ds(NK * XB * 8 + 7, NK * XB, stride=8), :]

    copy_bytes(raw, raw_sem).wait()
    low = lax.broadcasted_iota(jnp.int32, (COLS, 128), 1) < ROWS

    def pack(j, carry):
        lanes = pl.ds(pl.multiple_of(128 * j, 128), 128)
        for f in range(2):
            first = raw[f, 0, :, lanes]
            second = raw[f, 1, :, lanes]
            packed[2 * j, f] = jnp.where(low, first, pltpu.roll(second, ROWS, 1))
            packed[2 * j + 1, f] = jnp.where(low, pltpu.roll(first, ROWS, 1), second)
        return carry

    lax.fori_loop(0, STRIPS // 2, pack, 0)
    here = pl.ds(pl.multiple_of(PADX + COLS * me, 8), COLS)
    for f in range(2):
        field[f, here, :] = packed[me, f]

    pl.semaphore_wait(barrier, STRIPS - 1 + 2)

    halo_up = pltpu.make_async_remote_copy(
        halo_out.at[1], halo_in.at[0], halo_send.at[0], halo_recv.at[0],
        device_id=(next_strip, lag), device_id_type=MESH,
    )
    halo_down = pltpu.make_async_remote_copy(
        halo_out.at[0], halo_in.at[1], halo_send.at[1], halo_recv.at[1],
        device_id=(prev_strip, lag), device_id_type=MESH,
    )
    halo_up.start()
    halo_down.start()

    def send(d, carry):
        to = lax.rem(me + d, STRIPS)
        pltpu.make_async_remote_copy(
            packed.at[to], field.at[:, here, :], a2a_send, a2a_recv,
            device_id=(to, lag), device_id_type=MESH,
        ).start()
        return carry

    lax.fori_loop(1, STRIPS, send, 0)

    halo_up.wait()
    halo_down.wait()
    halo_in[0] = jnp.where(me == 0, 0.0, halo_in[0])
    halo_in[1] = jnp.where(me == STRIPS - 1, 0.0, halo_in[1])

    lane = lax.broadcasted_iota(jnp.int32, (ROWS, 128), 1)
    wide = lax.broadcasted_iota(jnp.int32, (128, 128), 1) < ROWS

    def filtered(k):
        centers = []
        for b in range(XB):
            tiles[k, b, 7:8, :] = halo_in[0, pl.ds(k * XB + b, 1), :]
            tiles[k, b, 8 + ROWS : 9 + ROWS, :] = halo_in[1, pl.ds(k * XB + b, 1), :]
        out = []
        for b in range(XB):
            center = tiles[k, b, 8 : 8 + ROWS, :]
            above = tiles[k, b, 7 : 7 + ROWS, :]
            below = tiles[k, b, 9 : 9 + ROWS, :]
            left = pltpu.roll(center, 1, 1)
            right = pltpu.roll(center, 127, 1)
            before = (
                pltpu.roll(tiles[k, b - 1, 8 : 8 + ROWS, :], 1, 1) if b else jnp.zeros_like(left)
            )
            after = (
                pltpu.roll(tiles[k, b + 1, 8 : 8 + ROWS, :], 127, 1)
                if b < XB - 1
                else jnp.zeros_like(left)
            )
            left = jnp.where(lane == 0, before, left)
            right = jnp.where(lane == 127, after, right)
            out.append(2.0 * center - 0.25 * ((above + below) + (left + right)))
        return out

    def pair(p, carry):
        one = filtered(2 * p)
        two = filtered(2 * p + 1)
        for b in range(XB):
            both = jnp.concatenate([one[b], two[b]], axis=0).T
            turned = pltpu.roll(both, ROWS, 1)
            base = PADF + 2 * p * NX + 128 * b
            filt[pl.ds(pl.multiple_of(base, 8), 128), :] = jnp.where(wide, both, turned)
            filt[pl.ds(pl.multiple_of(base + NX, 8), 128), :] = jnp.where(wide, turned, both)
        return carry

    for c in range(CHUNKS):
        copy_bytes(tiles.at[c * KC : (c + 1) * KC, :, 8 : 8 + ROWS, :], load_sem.at[c]).wait()
        lax.fori_loop(c * KC // 2, (c + 1) * KC // 2, pair, 0)

    copy_bytes(packed.at[0 : STRIPS - 1], a2a_recv).wait()

    first_lag = lag * NK - NK * LAGS // 2

    def products(block, put):
        def sub(i, carry):
            x = block * OUTX + i * SUB

            def step(k, sums):
                h = first_lag + k
                at = PADF + k * NX + x
                s = sums[0] + filt[pl.ds(at + h, SUB), :] * field[1, pl.ds(PADX + x + 2 * h, SUB), :]
                r = sums[1] + filt[pl.ds(at - h, SUB), :] * field[0, pl.ds(PADX + x - 2 * h, SUB), :]
                return s, r

            zero = jnp.zeros((SUB, 128), F32)
            s, r = lax.fori_loop(0, NK, step, (zero, zero), unroll=4)
            put(pl.ds(pl.multiple_of(i * SUB, SUB), SUB), s, r)
            return carry

        lax.fori_loop(0, OUTX // SUB, sub, 0)

    def put_part(n):
        def put(rows, s, r):
            part[n, 0, rows, :] = s
            part[n, 1, rows, :] = r

        return put

    def lag_copy(n, src, dst, to):
        return pltpu.make_async_remote_copy(
            src, dst, rs_send.at[n], rs_recv.at[n], device_id=(me, to), device_id_type=MESH
        )

    products(lax.rem(lag + 2, LAGS), put_part(0))
    far_s = lag_copy(0, part.at[0, 0], relay.at[0], up_lag)
    far_r = lag_copy(1, part.at[0, 1], relay.at[1], down_lag)
    far_s.start()
    far_r.start()
    products(up_lag, put_part(1))
    up_r = lag_copy(2, part.at[1, 1], near_in.at[0, 1], up_lag)
    up_r.start()
    products(down_lag, put_part(2))
    down_s = lag_copy(3, part.at[2, 0], near_in.at[1, 0], down_lag)
    down_s.start()

    far_s.wait_recv()
    part[1, 0] = part[1, 0] + relay[0]
    up_s = lag_copy(4, part.at[1, 0], near_in.at[0, 0], up_lag)
    up_s.start()
    far_r.wait_recv()
    part[2, 1] = part[2, 1] + relay[1]
    down_r = lag_copy(5, part.at[2, 1], near_in.at[1, 1], down_lag)
    down_r.start()

    def put_own(rows, s, r):
        own[0, rows, :] = s
        own[1, rows, :] = r

    products(lag, put_own)

    for f, out, copies in ((0, out_s, (down_s, up_s)), (1, out_r, (up_r, down_r))):
        for copy in copies:
            copy.wait_recv()
        for b in range(OUTX // 128):
            rows = pl.ds(128 * b, 128)
            total = own[f, rows, :] + near_in[0, f, rows, :] + near_in[1, f, rows, :]
            turned = total.T
            out[0, :, rows] = turned[0:ROWS]
            out[1, :, rows] = turned[ROWS:]

    for copy in (far_s, far_r, up_r, down_s, up_s, down_r):
        copy.wait_send()
    copy_bytes(packed.at[0 : STRIPS - 1], a2a_send).wait()


def local(image_grad, source_field, receiver_field):
    vmem = pltpu.VMEM
    dma = pltpu.SemaphoreType.DMA
    out = jax.ShapeDtypeStruct((2, ROWS, OUTX), F32)
    return pl.pallas_call(
        kernel,
        out_shape=(out, out),
        in_specs=[pl.BlockSpec(memory_space=pl.ANY)] * 3,
        out_specs=[pl.BlockSpec(memory_space=pltpu.VMEM)] * 2,
        scratch_shapes=[
            vmem((2, NK, XB, 8, 128), F32),
            vmem((NK, XB, SLOT, 128), F32),
            vmem((NK * NX + 2 * PADF, 128), F32),
            vmem((STRIPS, 2, COLS, 128), F32),
            vmem((2, 2, COLS, STRIPS * ROWS), F32),
            vmem((2, NX + 2 * PADX, 128), F32),
            vmem((2, NK * XB, 128), F32),
            vmem((2, NK * XB, 128), F32),
            vmem((3, 2, OUTX, 128), F32),
            vmem((2, OUTX, 128), F32),
            vmem((2, 2, OUTX, 128), F32),
            vmem((2, OUTX, 128), F32),
            dma,
            dma,
            dma((CHUNKS,)),
            dma,
            dma,
            dma((2,)),
            dma((2,)),
            dma((6,)),
            dma((6,)),
        ],
        compiler_params=pltpu.CompilerParams(
            collective_id=0, has_side_effects=True, vmem_limit_bytes=60 << 20
        ),
        name="adjoint",
    )(image_grad, jnp.swapaxes(source_field, 1, 2), jnp.swapaxes(receiver_field, 1, 2))


def solution(mesh):
    in_specs = (P("lag", "strip", None), P(None, None, "strip"), P(None, None, "strip"))
    out_specs = (P(None, "strip", "lag"), P(None, "strip", "lag"))
    return jax.shard_map(local, mesh=mesh, in_specs=in_specs, out_specs=out_specs, check_vma=False)
```

```python
import jax
import jax.numpy as jnp
from jax import lax
from jax.experimental import pallas as pl
from jax.experimental.pallas import tpu as pltpu
from jax.sharding import PartitionSpec as P

MESH = pl.DeviceIdType.MESH
F32 = jnp.float32

STRIPS = 64
LAGS = 4
NK = 32
PAIRS = NK // 2
ROWS = 64
NX = 1024
XB = NX // 128
COLS = NX // STRIPS
PADL = 16
PADX = 136
PADF = 72
SLOT = 80
OUTX = NX // LAGS
SUB = 128
SUBX = SUB + 8
EXP = 80
CHUNKS = 8
KC = NK // CHUNKS


def copy_bytes(ref, sem):
    return pltpu.make_async_copy(ref, ref, sem)


def kernel(
    grad, source, receiver, out_s, out_r,
    edge, tiles, filt, packed, raw, land, field, halo_out, halo_in,
    sums, part, relay, near_in, own,
    edge_sem, raw_sem, load_sem, a2a_send, a2a_recv,
    halo_send, halo_recv, rs_send, rs_recv,
):
    me = lax.axis_index("strip")
    lag = lax.axis_index("lag")
    up_lag = lax.rem(lag + 1, LAGS)
    down_lag = lax.rem(lag + LAGS - 1, LAGS)
    next_strip = lax.rem(me + 1, STRIPS)
    prev_strip = lax.rem(me + STRIPS - 1, STRIPS)
    my_y, my_x, my_z, my_core = me // 16, (me // 4) % 4, (me // 2) % 2, me % 2

    def peer(i):
        y = lax.rem(my_y + i // 16, 4)
        x = lax.rem(my_x + (i // 4) % 4, 4)
        z = lax.rem(my_z + (i // 2) % 2, 2)
        core = lax.rem(my_core + i % 2, 2)
        return ((y * 4 + x) * 2 + z) * 2 + core, (i // 2) % 2, core

    def sender_lag(cross, core):
        side = lax.rem(lag + LAGS - 1 + 2 * my_z, LAGS)
        return jnp.where(cross * core == 1, side, lag)

    def target_lag(cross):
        side = lax.rem(lag + LAGS - 1 + 2 * my_z, LAGS)
        return jnp.where(cross * my_core == 1, side, lag)

    barrier = pltpu.get_barrier_semaphore()

    def greet(i, carry):
        strip, cross, core = peer(i)
        pl.semaphore_signal(
            barrier, inc=1, device_id=(strip, sender_lag(cross, core)), device_id_type=MESH
        )
        return carry

    for other in (up_lag, down_lag):
        pl.semaphore_signal(barrier, inc=1, device_id=(me, other), device_id_type=MESH)
    for other in (next_strip, prev_strip):
        pl.semaphore_signal(barrier, inc=1, device_id=(other, lag), device_id_type=MESH)
    lax.fori_loop(1, STRIPS, greet, 0)

    pltpu.make_async_copy(receiver, raw.at[1], raw_sem.at[1]).start()
    for b in range(XB):
        lanes = pl.ds(128 * b, 128)
        pltpu.make_async_copy(grad.at[:, 0:8, lanes], edge.at[0, :, b], edge_sem).start()
        pltpu.make_async_copy(
            grad.at[:, ROWS - 8 : ROWS, lanes], edge.at[1, :, b], edge_sem
        ).start()
    pltpu.make_async_copy(source, raw.at[0], raw_sem.at[0]).start()
    for c in range(CHUNKS):
        for b in range(XB):
            pltpu.make_async_copy(
                grad.at[c * KC : (c + 1) * KC, :, 128 * b : 128 * (b + 1)],
                tiles.at[c * KC : (c + 1) * KC, b, 8 : 8 + ROWS, :],
                load_sem.at[c],
            ).start()

    low = lax.broadcasted_iota(jnp.int32, (COLS, 128), 1) < ROWS

    def pack(f):
        def one(j, carry):
            lanes = pl.ds(pl.multiple_of(128 * j, 128), 128)
            first = raw[f, 0, :, lanes]
            second = raw[f, 1, :, lanes]
            packed[f, 2 * j] = jnp.where(low, first, pltpu.roll(second, ROWS, 1))
            packed[f, 2 * j + 1] = jnp.where(low, pltpu.roll(first, ROWS, 1), second)
            return carry

        copy_bytes(raw.at[f], raw_sem.at[f]).wait()
        lax.fori_loop(0, STRIPS // 2, one, 0, unroll=4)

    pack(1)

    copy_bytes(edge, edge_sem).wait()
    flat = edge.reshape(2 * NK * XB * 8, 128)
    halo_out[0] = flat[pl.ds(0, NK * XB, stride=8), :]
    halo_out[1] = flat[pl.ds(NK * XB * 8 + 7, NK * XB, stride=8), :]

    here = pl.ds(pl.multiple_of(PADL + COLS * me, 8), COLS)

    def send_field(f):
        def send(i, carry):
            strip, cross, core = peer(i)
            pltpu.make_async_remote_copy(
                packed.at[f, strip], land.at[f, here, :], a2a_send.at[f], a2a_recv.at[f],
                device_id=(strip, target_lag(cross)), device_id_type=MESH,
            ).start()
            return carry

        lax.fori_loop(1, STRIPS, send, 0)

    pl.semaphore_wait(barrier, STRIPS - 1 + 4)

    halo_up = pltpu.make_async_remote_copy(
        halo_out.at[1], halo_in.at[0], halo_send.at[0], halo_recv.at[0],
        device_id=(next_strip, lag), device_id_type=MESH,
    )
    halo_down = pltpu.make_async_remote_copy(
        halo_out.at[0], halo_in.at[1], halo_send.at[1], halo_recv.at[1],
        device_id=(prev_strip, lag), device_id_type=MESH,
    )
    halo_up.start()
    halo_down.start()
    send_field(1)
    pack(0)
    send_field(0)

    for f in range(2):
        land[f, 0:PADL, :] = jnp.zeros((PADL, 128), F32)
        land[f, PADL + NX :, :] = jnp.zeros((PADL, 128), F32)
        land[f, here, :] = packed[f, me]
        for t in range(2):
            field[f, t, 0:PADX, :] = jnp.zeros((PADX, 128), F32)
            field[f, t, PADX + NX :, :] = jnp.zeros((PADX, 128), F32)
    filt[0:PADF, :] = jnp.zeros((PADF, 128), F32)
    filt[PADF + PAIRS * NX :, :] = jnp.zeros((PADF, 128), F32)

    halo_up.wait()
    halo_down.wait()
    halo_in[0] = jnp.where(me == 0, 0.0, halo_in[0])
    halo_in[1] = jnp.where(me == STRIPS - 1, 0.0, halo_in[1])

    lane = lax.broadcasted_iota(jnp.int32, (ROWS, 128), 1)

    def filtered(k):
        for b in range(XB):
            tiles[k, b, 7:8, :] = halo_in[0, pl.ds(k * XB + b, 1), :]
            tiles[k, b, 8 + ROWS : 9 + ROWS, :] = halo_in[1, pl.ds(k * XB + b, 1), :]
        centers = [tiles[k, b, 8 : 8 + ROWS, :] for b in range(XB)]
        lefts = [pltpu.roll(c, 1, 1) for c in centers]
        rights = [pltpu.roll(c, 127, 1) for c in centers]
        none = jnp.zeros((ROWS, 128), F32)
        out = []
        for b in range(XB):
            above = tiles[k, b, 7 : 7 + ROWS, :]
            below = tiles[k, b, 9 : 9 + ROWS, :]
            left = jnp.where(lane == 0, lefts[b - 1] if b else none, lefts[b])
            right = jnp.where(lane == 127, rights[b + 1] if b < XB - 1 else none, rights[b])
            out.append(8.0 * centers[b] - ((above + below) + (left + right)))
        return out

    def pair(p, carry):
        one = filtered(2 * p)
        two = filtered(2 * p + 1)
        for b in range(XB):
            base = pl.multiple_of(PADF + p * NX + 128 * b, 8)
            filt[pl.ds(base, 128), :] = jnp.concatenate([one[b], two[b]], axis=0).T
        return carry

    for c in range(CHUNKS):
        copy_bytes(tiles.at[c * KC : (c + 1) * KC, :, 8 : 8 + ROWS, :], load_sem.at[c]).wait()
        lax.fori_loop(c * KC // 2, (c + 1) * KC // 2, pair, 0)

    first_lag = lag * NK - NK * LAGS // 2

    def lag_copy(n, src, dst, to):
        return pltpu.make_async_remote_copy(
            src, dst, rs_send.at[n], rs_recv.at[n], device_id=(me, to), device_id_type=MESH
        )

    def adjoint(f):
        sign = 1 if f == 1 else -1
        copy_bytes(packed.at[f, 0 : STRIPS - 1], a2a_recv.at[f]).wait()

        wide = lax.broadcasted_iota(jnp.int32, (EXP, 128), 1) < ROWS

        def expand(i, carry):
            at = pl.multiple_of(PADL - 8 + i * EXP, 8)
            this = land[f, pl.ds(at, EXP), :]
            other = land[f, pl.ds(at + sign, EXP), :]
            to = pl.ds(pl.multiple_of(PADX - 8 + i * EXP, 8), EXP)
            field[f, 0, to, :] = jnp.where(wide, this, pltpu.roll(other, ROWS, 1))
            field[f, 1, to, :] = jnp.where(wide, pltpu.roll(this, ROWS, 1), other)
            return carry

        lax.fori_loop(0, (NX + 16) // EXP, expand, 0)

        half = lax.broadcasted_iota(jnp.int32, (SUB, 128), 1) < ROWS
        start = 0 if sign == 1 else -8

        def products(block, i, out):
            x = block * OUTX + i * SUB + start

            def step(p, totals):
                h = (first_lag + 2 * p) * sign
                g = filt[pl.ds(PADF + p * NX + x + h, SUBX), :]
                rows = pl.ds(PADX + x + 2 * h, SUBX)
                return totals[0] + g * field[f, 0, rows, :], totals[1] + g * field[f, 1, rows, :]

            zero = jnp.zeros((SUBX, 128), F32)
            a, b = lax.fori_loop(0, PAIRS, step, (zero, zero), unroll=2)
            sums[0] = a
            sums[1] = b
            own_at = 0 if sign == 1 else 8
            a, b = sums[0, own_at : own_at + SUB], sums[1, own_at : own_at + SUB]
            own_at += sign
            c, d = sums[0, own_at : own_at + SUB], sums[1, own_at : own_at + SUB]
            out[...] = jnp.where(half, a, pltpu.roll(b, ROWS, 1)) + jnp.where(
                half, pltpu.roll(c, ROWS, 1), d
            )

        far = lax.rem(lag + 2, LAGS)
        products(far, 0, part.at[f, 0, 0])
        far_up = lag_copy(6 * f, part.at[f, 0, 0], relay.at[f, 0], up_lag)
        far_up.start()
        products(far, 1, part.at[f, 0, 1])
        far_down = lag_copy(6 * f + 1, part.at[f, 0, 1], relay.at[f, 1], down_lag)
        far_down.start()
        products(up_lag, 1, part.at[f, 1, 1])
        up_1 = lag_copy(6 * f + 2, part.at[f, 1, 1], near_in.at[f, 0, 1], up_lag)
        up_1.start()
        products(down_lag, 0, part.at[f, 2, 0])
        down_0 = lag_copy(6 * f + 3, part.at[f, 2, 0], near_in.at[f, 1, 0], down_lag)
        down_0.start()
        products(up_lag, 0, part.at[f, 1, 0])
        products(down_lag, 1, part.at[f, 2, 1])
        products(lag, 0, own.at[f, 0])
        products(lag, 1, own.at[f, 1])
        far_up.wait_recv()
        part[f, 1, 0] = part[f, 1, 0] + relay[f, 0]
        up_0 = lag_copy(6 * f + 4, part.at[f, 1, 0], near_in.at[f, 0, 0], up_lag)
        up_0.start()
        far_down.wait_recv()
        part[f, 2, 1] = part[f, 2, 1] + relay[f, 1]
        down_1 = lag_copy(6 * f + 5, part.at[f, 2, 1], near_in.at[f, 1, 1], down_lag)
        down_1.start()
        return far_up, far_down, up_1, down_0, up_0, down_1

    def finish(f, out, copies):
        far_up, far_down, up_1, down_0, up_0, down_1 = copies
        for copy in (up_1, down_0, up_0, down_1):
            copy.wait_recv()
        for b in range(OUTX // 128):
            total = own[f, b] + near_in[f, 0, b] + near_in[f, 1, b]
            turned = (0.25 * total).T
            lanes = pl.ds(128 * b, 128)
            out[0, :, lanes] = turned[0:ROWS]
            out[1, :, lanes] = turned[ROWS:]

    copies_s = adjoint(1)
    copies_r = adjoint(0)
    finish(1, out_s, copies_s)
    finish(0, out_r, copies_r)

    for copy in copies_s + copies_r:
        copy.wait_send()
    for f in range(2):
        copy_bytes(packed.at[f, 0 : STRIPS - 1], a2a_send.at[f]).wait()


def local(image_grad, source_field, receiver_field):
    vmem = pltpu.VMEM
    dma = pltpu.SemaphoreType.DMA
    out = jax.ShapeDtypeStruct((2, ROWS, OUTX), F32)
    return pl.pallas_call(
        kernel,
        out_shape=(out, out),
        in_specs=[pl.BlockSpec(memory_space=pl.ANY)] * 3,
        out_specs=[pl.BlockSpec(memory_space=pltpu.VMEM)] * 2,
        scratch_shapes=[
            vmem((2, NK, XB, 8, 128), F32),
            vmem((NK, XB, SLOT, 128), F32),
            vmem((PAIRS * NX + 2 * PADF, 128), F32),
            vmem((2, STRIPS, COLS, 128), F32),
            vmem((2, 2, COLS, STRIPS * ROWS), F32),
            vmem((2, NX + 2 * PADL, 128), F32),
            vmem((2, 2, NX + 2 * PADX, 128), F32),
            vmem((2, NK * XB, 128), F32),
            vmem((2, NK * XB, 128), F32),
            vmem((2, SUBX, 128), F32),
            vmem((2, 3, 2, SUB, 128), F32),
            vmem((2, 2, SUB, 128), F32),
            vmem((2, 2, 2, SUB, 128), F32),
            vmem((2, 2, SUB, 128), F32),
            dma,
            dma((2,)),
            dma((CHUNKS,)),
            dma((2,)),
            dma((2,)),
            dma((2,)),
            dma((2,)),
            dma((12,)),
            dma((12,)),
        ],
        compiler_params=pltpu.CompilerParams(
            collective_id=0, has_side_effects=True, vmem_limit_bytes=60 << 20
        ),
        name="adjoint",
    )(image_grad, jnp.swapaxes(source_field, 1, 2), jnp.swapaxes(receiver_field, 1, 2))


def solution(mesh):
    in_specs = (P("lag", "strip", None), P(None, None, "strip"), P(None, None, "strip"))
    out_specs = (P(None, "strip", "lag"), P(None, "strip", "lag"))
    return jax.shard_map(local, mesh=mesh, in_specs=in_specs, out_specs=out_specs, check_vma=False)
```

```python
import jax
import jax.numpy as jnp
from jax import lax
from jax.experimental import pallas as pl
from jax.experimental.pallas import tpu as pltpu
from jax.sharding import PartitionSpec as P

MESH = pl.DeviceIdType.MESH
F32 = jnp.float32

STRIPS = 64
LAGS = 4
NK = 32
PAIRS = NK // 2
ROWS = 64
NX = 1024
XB = NX // 128
COLS = NX // STRIPS
PADL = 16
PADX = 136
PADF = 72
SLOT = 80
OUTX = NX // LAGS
SUB = 128
SUBX = SUB + 8
EXP = 80
CHUNKS = 8
KC = NK // CHUNKS


def copy_bytes(ref, sem):
    return pltpu.make_async_copy(ref, ref, sem)


def kernel(
    grad, source, receiver, out_s, out_r,
    edge, tiles, smooth, columns, filt, packed, raw, land, field, halo_out, halo_in,
    sums, part, relay, near_in, own,
    edge_sem, raw_sem, load_sem, a2a_send, a2a_recv,
    halo_send, halo_recv, rs_send, rs_recv,
):
    me = lax.axis_index("strip")
    lag = lax.axis_index("lag")
    up_lag = lax.rem(lag + 1, LAGS)
    down_lag = lax.rem(lag + LAGS - 1, LAGS)
    next_strip = lax.rem(me + 1, STRIPS)
    prev_strip = lax.rem(me + STRIPS - 1, STRIPS)
    chip, my_z, my_core = lax.div(me, 4), lax.rem(lax.div(me, 2), 2), lax.rem(me, 2)

    side = lax.rem(lag + LAGS - 1 + 2 * my_z, LAGS)
    crossing = [jnp.where(my_z == z, lag, side) for z in range(2)]
    sender_lag = [lag, crossing[0], lag, crossing[1]]
    target_lag = [jnp.where(my_core == 1, crossing[e // 2], lag) for e in range(4)]

    def each_peer(lags, act):
        def others(j, carry):
            base = lax.rem(chip + j, STRIPS // 4) * 4
            for e in range(4):
                act(base + e, lags[e])
            return carry

        lax.fori_loop(1, STRIPS // 4, others, 0)
        for e in range(1, 4):
            place = lax.rem(lax.rem(me, 4) + e, 4)
            to = lags[0]
            for n in range(1, 4):
                to = jnp.where(place == n, lags[n], to)
            act(chip * 4 + place, to)

    barrier = pltpu.get_barrier_semaphore()

    def greet(strip, to):
        pl.semaphore_signal(barrier, inc=1, device_id=(strip, to), device_id_type=MESH)

    each_peer(sender_lag, greet)
    for other in (up_lag, down_lag):
        greet(me, other)
    for other in (next_strip, prev_strip):
        greet(other, lag)

    pltpu.make_async_copy(receiver, raw.at[1], raw_sem.at[1]).start()
    for b in range(XB):
        lanes = pl.ds(128 * b, 128)
        pltpu.make_async_copy(grad.at[:, 0:8, lanes], edge.at[0, :, b], edge_sem).start()
        pltpu.make_async_copy(
            grad.at[:, ROWS - 8 : ROWS, lanes], edge.at[1, :, b], edge_sem
        ).start()
    pltpu.make_async_copy(source, raw.at[0], raw_sem.at[0]).start()
    by_lag = tiles.reshape(NK, XB, SLOT, 128)
    for c in range(CHUNKS):
        for b in range(XB):
            pltpu.make_async_copy(
                grad.at[c * KC : (c + 1) * KC, :, 128 * b : 128 * (b + 1)],
                by_lag.at[c * KC : (c + 1) * KC, b, 8 : 8 + ROWS, :],
                load_sem.at[c],
            ).start()

    low = lax.broadcasted_iota(jnp.int32, (COLS, 128), 1) < ROWS

    def pack(f):
        def one(j, carry):
            lanes = pl.ds(pl.multiple_of(128 * j, 128), 128)
            first = raw[f, 0, :, lanes]
            second = raw[f, 1, :, lanes]
            packed[f, 2 * j] = jnp.where(low, first, pltpu.roll(second, ROWS, 1))
            packed[f, 2 * j + 1] = jnp.where(low, pltpu.roll(first, ROWS, 1), second)
            return carry

        copy_bytes(raw.at[f], raw_sem.at[f]).wait()
        lax.fori_loop(0, STRIPS // 2, one, 0, unroll=4)

    pack(1)

    copy_bytes(edge, edge_sem).wait()
    flat = edge.reshape(2 * NK * XB * 8, 128)
    halo_out[0] = flat[pl.ds(0, NK * XB, stride=8), :]
    halo_out[1] = flat[pl.ds(NK * XB * 8 + 7, NK * XB, stride=8), :]

    here = pl.ds(pl.multiple_of(PADL + COLS * me, 8), COLS)

    def send_field(f):
        def send(strip, to):
            pltpu.make_async_remote_copy(
                packed.at[f, strip], land.at[f, here, :], a2a_send.at[f], a2a_recv.at[f],
                device_id=(strip, to), device_id_type=MESH,
            ).start()

        each_peer(target_lag, send)

    pl.semaphore_wait(barrier, STRIPS - 1 + 4)

    halo_up = pltpu.make_async_remote_copy(
        halo_out.at[1], halo_in.at[0], halo_send.at[0], halo_recv.at[0],
        device_id=(next_strip, lag), device_id_type=MESH,
    )
    halo_down = pltpu.make_async_remote_copy(
        halo_out.at[0], halo_in.at[1], halo_send.at[1], halo_recv.at[1],
        device_id=(prev_strip, lag), device_id_type=MESH,
    )
    halo_up.start()
    halo_down.start()
    send_field(1)
    pack(0)
    send_field(0)

    for f in range(2):
        land[f, 0:PADL, :] = jnp.zeros((PADL, 128), F32)
        land[f, PADL + NX :, :] = jnp.zeros((PADL, 128), F32)
        land[f, here, :] = packed[f, me]
        for t in range(2):
            field[f, t, 0:PADX, :] = jnp.zeros((PADX, 128), F32)
            field[f, t, PADX + NX :, :] = jnp.zeros((PADX, 128), F32)
    filt[0:PADF, :] = jnp.zeros((PADF, 128), F32)
    filt[PADF + PAIRS * NX :, :] = jnp.zeros((PADF, 128), F32)

    tile_rows = tiles.reshape(NK * XB * SLOT, 128)
    blank = jnp.zeros((NK * XB, 128), F32)
    for row in (7, 8 + ROWS):
        tile_rows[pl.ds(row, NK * XB, stride=SLOT), :] = blank

    def prepare(p, carry):
        columns[p, 0:8, :] = jnp.zeros((8, 128), F32)
        columns[p, 8 + NX :, :] = jnp.zeros((8, 128), F32)
        for b in range(XB):
            centers = []
            for n in range(2):
                j = (2 * p + n) * XB + b
                center = tiles[j, 8 : 8 + ROWS, :]
                above = tiles[j, 7 : 7 + ROWS, :]
                below = tiles[j, 9 : 9 + ROWS, :]
                smooth[j] = 8.0 * center - (above + below)
                centers.append(center)
            columns[p, 8 + 128 * b : 136 + 128 * b, :] = jnp.concatenate(centers, axis=0).T
        return carry

    for c in range(CHUNKS):
        at = pl.ds(c * KC * XB, KC * XB)
        copy_bytes(tiles.at[at, 8 : 8 + ROWS, :], load_sem.at[c]).wait()
        lax.fori_loop(c * KC // 2, (c + 1) * KC // 2, prepare, 0)

    halo_up.wait()
    halo_down.wait()
    smooth_rows = smooth.reshape(NK * XB * ROWS, 128)
    first = pl.ds(0, NK * XB, stride=ROWS)
    last = pl.ds(ROWS - 1, NK * XB, stride=ROWS)
    smooth_rows[first, :] = smooth_rows[first, :] - jnp.where(me == 0, 0.0, halo_in[0])
    smooth_rows[last, :] = smooth_rows[last, :] - jnp.where(me == STRIPS - 1, 0.0, halo_in[1])

    def turn(p, carry):
        for b in range(XB):
            both = [smooth[(2 * p + n) * XB + b] for n in range(2)]
            sides = columns[p, 7 + 128 * b : 135 + 128 * b, :] + columns[p, 9 + 128 * b : 137 + 128 * b, :]
            base = pl.multiple_of(PADF + p * NX + 128 * b, 8)
            filt[pl.ds(base, 128), :] = jnp.concatenate(both, axis=0).T - sides
        return carry

    lax.fori_loop(0, PAIRS, turn, 0)

    first_lag = lag * NK - NK * LAGS // 2

    def lag_copy(n, src, dst, to):
        return pltpu.make_async_remote_copy(
            src, dst, rs_send.at[n], rs_recv.at[n], device_id=(me, to), device_id_type=MESH
        )

    def adjoint(f, between):
        sign = 1 if f == 1 else -1
        copy_bytes(packed.at[f, 0 : STRIPS - 1], a2a_recv.at[f]).wait()

        wide = lax.broadcasted_iota(jnp.int32, (EXP, 128), 1) < ROWS

        def expand(i, carry):
            at = pl.multiple_of(PADL - 8 + i * EXP, 8)
            this = land[f, pl.ds(at, EXP), :]
            other = land[f, pl.ds(at + sign, EXP), :]
            to = pl.ds(pl.multiple_of(PADX - 8 + i * EXP, 8), EXP)
            field[f, 0, to, :] = jnp.where(wide, this, pltpu.roll(other, ROWS, 1))
            field[f, 1, to, :] = jnp.where(wide, pltpu.roll(this, ROWS, 1), other)
            return carry

        lax.fori_loop(0, (NX + 16) // EXP, expand, 0)

        half = lax.broadcasted_iota(jnp.int32, (SUB, 128), 1) < ROWS
        start = 0 if sign == 1 else -8

        def products(block, i, out):
            x = block * OUTX + i * SUB + start

            def step(p, totals):
                h = (first_lag + 2 * p) * sign
                g = filt[pl.ds(PADF + p * NX + x + h, SUBX), :]
                rows = pl.ds(PADX + x + 2 * h, SUBX)
                return totals[0] + g * field[f, 0, rows, :], totals[1] + g * field[f, 1, rows, :]

            zero = jnp.zeros((SUBX, 128), F32)
            a, b = lax.fori_loop(0, PAIRS, step, (zero, zero), unroll=4)
            sums[0] = a
            sums[1] = b
            own_at = 0 if sign == 1 else 8
            a, b = sums[0, own_at : own_at + SUB], sums[1, own_at : own_at + SUB]
            own_at += sign
            c, d = sums[0, own_at : own_at + SUB], sums[1, own_at : own_at + SUB]
            out[...] = jnp.where(half, a, pltpu.roll(b, ROWS, 1)) + jnp.where(
                half, pltpu.roll(c, ROWS, 1), d
            )

        far = lax.rem(lag + 2, LAGS)
        products(far, 0, part.at[f, 0, 0])
        far_up = lag_copy(6 * f, part.at[f, 0, 0], relay.at[f, 0], up_lag)
        far_up.start()
        products(far, 1, part.at[f, 0, 1])
        far_down = lag_copy(6 * f + 1, part.at[f, 0, 1], relay.at[f, 1], down_lag)
        far_down.start()
        between()
        products(up_lag, 1, part.at[f, 1, 1])
        up_1 = lag_copy(6 * f + 2, part.at[f, 1, 1], near_in.at[f, 0, 1], up_lag)
        up_1.start()
        products(down_lag, 0, part.at[f, 2, 0])
        down_0 = lag_copy(6 * f + 3, part.at[f, 2, 0], near_in.at[f, 1, 0], down_lag)
        down_0.start()
        products(up_lag, 0, part.at[f, 1, 0])
        products(down_lag, 1, part.at[f, 2, 1])
        products(lag, 0, own.at[f, 0])
        products(lag, 1, own.at[f, 1])
        up_0 = lag_copy(6 * f + 4, part.at[f, 1, 0], near_in.at[f, 0, 0], up_lag)
        down_1 = lag_copy(6 * f + 5, part.at[f, 2, 1], near_in.at[f, 1, 1], down_lag)
        return far_up, far_down, up_1, down_0, up_0, down_1

    def pass_on(f, copies):
        far_up, far_down, _, _, up_0, down_1 = copies
        far_up.wait_recv()
        part[f, 1, 0] = part[f, 1, 0] + relay[f, 0]
        up_0.start()
        far_down.wait_recv()
        part[f, 2, 1] = part[f, 2, 1] + relay[f, 1]
        down_1.start()

    def finish(f, out, copies):
        far_up, far_down, up_1, down_0, up_0, down_1 = copies
        for copy in (up_1, down_0, up_0, down_1):
            copy.wait_recv()
        for b in range(OUTX // 128):
            total = own[f, b] + near_in[f, 0, b] + near_in[f, 1, b]
            turned = (0.25 * total).T
            lanes = pl.ds(128 * b, 128)
            out[0, :, lanes] = turned[0:ROWS]
            out[1, :, lanes] = turned[ROWS:]

    copies_s = adjoint(1, lambda: None)
    copies_r = adjoint(0, lambda: pass_on(1, copies_s))
    pass_on(0, copies_r)
    finish(1, out_s, copies_s)
    finish(0, out_r, copies_r)

    for copy in copies_s + copies_r:
        copy.wait_send()
    for f in range(2):
        copy_bytes(packed.at[f, 0 : STRIPS - 1], a2a_send.at[f]).wait()


def local(image_grad, source_field, receiver_field):
    vmem = pltpu.VMEM
    dma = pltpu.SemaphoreType.DMA
    out = jax.ShapeDtypeStruct((2, ROWS, OUTX), F32)
    return pl.pallas_call(
        kernel,
        out_shape=(out, out),
        in_specs=[pl.BlockSpec(memory_space=pl.ANY)] * 3,
        out_specs=[pl.BlockSpec(memory_space=pltpu.VMEM)] * 2,
        scratch_shapes=[
            vmem((2, NK, XB, 8, 128), F32),
            vmem((NK * XB, SLOT, 128), F32),
            vmem((NK * XB, ROWS, 128), F32),
            vmem((PAIRS, NX + 16, 128), F32),
            vmem((PAIRS * NX + 2 * PADF, 128), F32),
            vmem((2, STRIPS, COLS, 128), F32),
            vmem((2, 2, COLS, STRIPS * ROWS), F32),
            vmem((2, NX + 2 * PADL, 128), F32),
            vmem((2, 2, NX + 2 * PADX, 128), F32),
            vmem((2, NK * XB, 128), F32),
            vmem((2, NK * XB, 128), F32),
            vmem((2, SUBX, 128), F32),
            vmem((2, 3, 2, SUB, 128), F32),
            vmem((2, 2, SUB, 128), F32),
            vmem((2, 2, 2, SUB, 128), F32),
            vmem((2, 2, SUB, 128), F32),
            dma,
            dma((2,)),
            dma((CHUNKS,)),
            dma((2,)),
            dma((2,)),
            dma((2,)),
            dma((2,)),
            dma((12,)),
            dma((12,)),
        ],
        compiler_params=pltpu.CompilerParams(
            collective_id=0, has_side_effects=True, vmem_limit_bytes=60 << 20
        ),
        name="adjoint",
    )(image_grad, jnp.swapaxes(source_field, 1, 2), jnp.swapaxes(receiver_field, 1, 2))


def solution(mesh):
    in_specs = (P("lag", "strip", None), P(None, None, "strip"), P(None, None, "strip"))
    out_specs = (P(None, "strip", "lag"), P(None, "strip", "lag"))
    return jax.shard_map(local, mesh=mesh, in_specs=in_specs, out_specs=out_specs, check_vma=False)
```

```python
import jax
import jax.numpy as jnp
from jax import lax
from jax.experimental import pallas as pl
from jax.experimental.pallas import tpu as pltpu
from jax.sharding import PartitionSpec as P

MESH = pl.DeviceIdType.MESH
F32 = jnp.float32

STRIPS = 64
LAGS = 4
NK = 32
PAIRS = NK // 2
ROWS = 64
NX = 1024
XB = NX // 128
COLS = NX // STRIPS
PADL = 16
PADX = 136
PADF = 72
SLOT = 80
OUTX = NX // LAGS
SUB = 128
SUBX = SUB + 8
EXP = 80
VMEM = 56000000
CHUNKS = 4
KC = NK // CHUNKS


def copy_bytes(ref, sem):
    return pltpu.make_async_copy(ref, ref, sem)


def kernel(
    grad, source, receiver, result,
    edge, tiles, smooth, columns, filt, packed, raw, land, field, halo_out, halo_in,
    sums, part, relay, near_in, own,
    edge_sem, raw_sem, load_sem, a2a_send, a2a_recv,
    halo_send, halo_recv, rs_send, rs_recv,
):
    me = lax.axis_index("strip")
    lag = lax.axis_index("lag")
    up_lag = lax.rem(lag + 1, LAGS)
    down_lag = lax.rem(lag + LAGS - 1, LAGS)
    next_strip = lax.rem(me + 1, STRIPS)
    prev_strip = lax.rem(me + STRIPS - 1, STRIPS)
    chip, my_z, my_core = lax.div(me, 4), lax.rem(lax.div(me, 2), 2), lax.rem(me, 2)

    side = lax.rem(lag + LAGS - 1 + 2 * my_z, LAGS)
    crossing = [jnp.where(my_z == z, lag, side) for z in range(2)]
    sender_lag = [lag, crossing[0], lag, crossing[1]]
    target_lag = [jnp.where(my_core == 1, crossing[e // 2], lag) for e in range(4)]

    def each_peer(lags, act):
        def others(j, carry):
            base = lax.rem(chip + j, STRIPS // 4) * 4
            for e in range(4):
                act(base + e, lags[e])
            return carry

        lax.fori_loop(1, STRIPS // 4, others, 0)
        for e in range(1, 4):
            place = lax.rem(lax.rem(me, 4) + e, 4)
            to = lags[0]
            for n in range(1, 4):
                to = jnp.where(place == n, lags[n], to)
            act(chip * 4 + place, to)

    barrier = pltpu.get_barrier_semaphore()

    def greet(strip, to):
        pl.semaphore_signal(barrier, inc=1, device_id=(strip, to), device_id_type=MESH)

    pltpu.make_async_copy(receiver, raw.at[1], raw_sem.at[1]).start()
    pltpu.make_async_copy(grad.at[:, 0:8, :], edge.at[0], edge_sem).start()
    pltpu.make_async_copy(grad.at[:, ROWS - 8 : ROWS, :], edge.at[1], edge_sem).start()
    pltpu.make_async_copy(source, raw.at[0], raw_sem.at[0]).start()

    each_peer(sender_lag, greet)
    for other in (up_lag, down_lag):
        greet(me, other)
    for other in (next_strip, prev_strip):
        greet(other, lag)

    by_lag = tiles.reshape(NK, XB, SLOT, 128)
    for c in range(CHUNKS):
        for b in range(XB):
            pltpu.make_async_copy(
                grad.at[c * KC : (c + 1) * KC, :, 128 * b : 128 * (b + 1)],
                by_lag.at[c * KC : (c + 1) * KC, b, 8 : 8 + ROWS, :],
                load_sem.at[c],
            ).start()

    low = lax.broadcasted_iota(jnp.int32, (COLS, 128), 1) < ROWS

    def pack(f):
        def one(j, carry):
            lanes = pl.ds(pl.multiple_of(128 * j, 128), 128)
            first = raw[f, 0, :, lanes]
            second = raw[f, 1, :, lanes]
            packed[f, 2 * j] = jnp.where(low, first, pltpu.roll(second, ROWS, 1))
            packed[f, 2 * j + 1] = jnp.where(low, pltpu.roll(first, ROWS, 1), second)
            return carry

        copy_bytes(raw.at[f], raw_sem.at[f]).wait()
        lax.fori_loop(0, STRIPS // 2, one, 0, unroll=4)

    pack(1)

    copy_bytes(edge, edge_sem).wait()
    for n in range(2):
        for b in range(XB):
            halo_out[n, b] = edge[n, :, 7 * n, 128 * b : 128 * (b + 1)]

    here = pl.ds(pl.multiple_of(PADL + COLS * me, 8), COLS)

    def send_field(f):
        def send(strip, to):
            pltpu.make_async_remote_copy(
                packed.at[f, strip], land.at[f, here, :], a2a_send.at[f], a2a_recv.at[f],
                device_id=(strip, to), device_id_type=MESH,
            ).start()

        each_peer(target_lag, send)

    pl.semaphore_wait(barrier, STRIPS - 1 + 4)

    halo_up = pltpu.make_async_remote_copy(
        halo_out.at[1], halo_in.at[0], halo_send.at[0], halo_recv.at[0],
        device_id=(next_strip, lag), device_id_type=MESH,
    )
    halo_down = pltpu.make_async_remote_copy(
        halo_out.at[0], halo_in.at[1], halo_send.at[1], halo_recv.at[1],
        device_id=(prev_strip, lag), device_id_type=MESH,
    )
    halo_up.start()
    halo_down.start()
    send_field(1)
    pack(0)
    send_field(0)

    for f in range(2):
        land[f, 0:PADL, :] = jnp.zeros((PADL, 128), F32)
        land[f, PADL + NX :, :] = jnp.zeros((PADL, 128), F32)
        land[f, here, :] = packed[f, me]
        for t in range(2):
            field[f, t, 0:PADX, :] = jnp.zeros((PADX, 128), F32)
            field[f, t, PADX + NX :, :] = jnp.zeros((PADX, 128), F32)
    filt[0:PADF, :] = jnp.zeros((PADF, 128), F32)
    filt[PADF + PAIRS * NX :, :] = jnp.zeros((PADF, 128), F32)

    tile_rows = tiles.reshape(NK * XB * SLOT, 128)
    blank = jnp.zeros((NK * XB, 128), F32)
    for row in (7, 8 + ROWS):
        tile_rows[pl.ds(row, NK * XB, stride=SLOT), :] = blank

    def prepare(p, carry):
        columns[p, 0:8, :] = jnp.zeros((8, 128), F32)
        columns[p, 8 + NX :, :] = jnp.zeros((8, 128), F32)
        for b in range(XB):
            centers = []
            for n in range(2):
                j = (2 * p + n) * XB + b
                center = tiles[j, 8 : 8 + ROWS, :]
                above = tiles[j, 7 : 7 + ROWS, :]
                below = tiles[j, 9 : 9 + ROWS, :]
                smooth[j] = 8.0 * center - (above + below)
                centers.append(center)
            columns[p, 8 + 128 * b : 136 + 128 * b, :] = jnp.concatenate(centers, axis=0).T
        return carry

    for c in range(CHUNKS):
        at = pl.ds(c * KC * XB, KC * XB)
        copy_bytes(tiles.at[at, 8 : 8 + ROWS, :], load_sem.at[c]).wait()
        lax.fori_loop(c * KC // 2, (c + 1) * KC // 2, prepare, 0)

    halo_up.wait()
    halo_down.wait()
    smooth_rows = smooth.reshape(NK * XB * ROWS, 128)
    for b in range(XB):
        first = pl.ds(ROWS * b, NK, stride=ROWS * XB)
        last = pl.ds(ROWS * b + ROWS - 1, NK, stride=ROWS * XB)
        above = jnp.where(me == 0, 0.0, halo_in[0, b])
        below = jnp.where(me == STRIPS - 1, 0.0, halo_in[1, b])
        smooth_rows[first, :] = smooth_rows[first, :] - above
        smooth_rows[last, :] = smooth_rows[last, :] - below

    def turn(p, carry):
        for b in range(XB):
            both = [smooth[(2 * p + n) * XB + b] for n in range(2)]
            sides = columns[p, 7 + 128 * b : 135 + 128 * b, :] + columns[p, 9 + 128 * b : 137 + 128 * b, :]
            base = pl.multiple_of(PADF + p * NX + 128 * b, 8)
            filt[pl.ds(base, 128), :] = jnp.concatenate(both, axis=0).T - sides
        return carry

    lax.fori_loop(0, PAIRS, turn, 0)

    first_lag = lag * NK - NK * LAGS // 2

    def lag_copy(n, src, dst, to):
        return pltpu.make_async_remote_copy(
            src, dst, rs_send.at[n], rs_recv.at[n], device_id=(me, to), device_id_type=MESH
        )

    def adjoint(f, between):
        sign = 1 if f == 1 else -1
        copy_bytes(packed.at[f, 0 : STRIPS - 1], a2a_recv.at[f]).wait()

        wide = lax.broadcasted_iota(jnp.int32, (EXP, 128), 1) < ROWS

        def expand(i, carry):
            at = pl.multiple_of(PADL - 8 + i * EXP, 8)
            this = land[f, pl.ds(at, EXP), :]
            other = land[f, pl.ds(at + sign, EXP), :]
            to = pl.ds(pl.multiple_of(PADX - 8 + i * EXP, 8), EXP)
            field[f, 0, to, :] = jnp.where(wide, this, pltpu.roll(other, ROWS, 1))
            field[f, 1, to, :] = jnp.where(wide, pltpu.roll(this, ROWS, 1), other)
            return carry

        lax.fori_loop(0, (NX + 16) // EXP, expand, 0)

        half = lax.broadcasted_iota(jnp.int32, (SUB, 128), 1) < ROWS
        start = 0 if sign == 1 else -8

        def products(block, i, out):
            x = block * OUTX + i * SUB + start

            def step(p, totals):
                h = (first_lag + 2 * p) * sign
                g = filt[pl.ds(PADF + p * NX + x + h, SUBX), :]
                rows = pl.ds(PADX + x + 2 * h, SUBX)
                return totals[0] + g * field[f, 0, rows, :], totals[1] + g * field[f, 1, rows, :]

            zero = jnp.zeros((SUBX, 128), F32)
            a, b = lax.fori_loop(0, PAIRS, step, (zero, zero), unroll=4)
            sums[0] = a
            sums[1] = b
            own_at = 0 if sign == 1 else 8
            a, b = sums[0, own_at : own_at + SUB], sums[1, own_at : own_at + SUB]
            own_at += sign
            c, d = sums[0, own_at : own_at + SUB], sums[1, own_at : own_at + SUB]
            out[...] = jnp.where(half, a, pltpu.roll(b, ROWS, 1)) + jnp.where(
                half, pltpu.roll(c, ROWS, 1), d
            )

        far = lax.rem(lag + 2, LAGS)
        products(far, 0, part.at[f, 0, 0])
        far_up = lag_copy(6 * f, part.at[f, 0, 0], relay.at[f, 0], up_lag)
        far_up.start()
        products(far, 1, part.at[f, 0, 1])
        far_down = lag_copy(6 * f + 1, part.at[f, 0, 1], relay.at[f, 1], down_lag)
        far_down.start()
        between()
        products(up_lag, 1, part.at[f, 1, 1])
        up_1 = lag_copy(6 * f + 2, part.at[f, 1, 1], near_in.at[f, 0, 1], up_lag)
        up_1.start()
        products(down_lag, 0, part.at[f, 2, 0])
        down_0 = lag_copy(6 * f + 3, part.at[f, 2, 0], near_in.at[f, 1, 0], down_lag)
        down_0.start()
        products(up_lag, 0, part.at[f, 1, 0])
        products(down_lag, 1, part.at[f, 2, 1])
        products(lag, 0, own.at[f, 0])
        products(lag, 1, own.at[f, 1])
        up_0 = lag_copy(6 * f + 4, part.at[f, 1, 0], near_in.at[f, 0, 0], up_lag)
        down_1 = lag_copy(6 * f + 5, part.at[f, 2, 1], near_in.at[f, 1, 1], down_lag)
        return far_up, far_down, up_1, down_0, up_0, down_1

    def pass_on(f, copies):
        far_up, far_down, _, _, up_0, down_1 = copies
        far_up.wait_recv()
        part[f, 1, 0] = part[f, 1, 0] + relay[f, 0]
        up_0.start()
        far_down.wait_recv()
        part[f, 2, 1] = part[f, 2, 1] + relay[f, 1]
        down_1.start()

    def finish(f, copies):
        far_up, far_down, up_1, down_0, up_0, down_1 = copies
        for copy in (up_1, down_0, up_0, down_1):
            copy.wait_recv()
        result[f] = 0.25 * (own[f] + near_in[f, 0] + near_in[f, 1])

    copies_s = adjoint(1, lambda: None)
    copies_r = adjoint(0, lambda: pass_on(1, copies_s))
    pass_on(0, copies_r)
    finish(1, copies_s)
    finish(0, copies_r)

    for copy in copies_s + copies_r:
        copy.wait_send()
    for f in range(2):
        copy_bytes(packed.at[f, 0 : STRIPS - 1], a2a_send.at[f]).wait()


def turned(result, out_s, out_r):
    for f, out in ((1, out_s), (0, out_r)):
        for b in range(OUTX // 128):
            lanes = pl.ds(128 * b, 128)
            block = result[f, b].T
            out[0, :, lanes] = block[0:ROWS]
            out[1, :, lanes] = block[ROWS:]


def local(image_grad, source_field, receiver_field):
    vmem = pltpu.VMEM
    dma = pltpu.SemaphoreType.DMA
    result = pl.pallas_call(
        kernel,
        out_shape=jax.ShapeDtypeStruct((2, OUTX // 128, 128, 128), F32),
        in_specs=[pl.BlockSpec(memory_space=pltpu.HBM)] * 3,
        out_specs=pl.BlockSpec(memory_space=pltpu.VMEM),
        scratch_shapes=[
            vmem((2, NK, 8, NX), F32),
            vmem((NK * XB, SLOT, 128), F32),
            vmem((NK * XB, ROWS, 128), F32),
            vmem((PAIRS, NX + 16, 128), F32),
            vmem((PAIRS * NX + 2 * PADF, 128), F32),
            vmem((2, STRIPS, COLS, 128), F32),
            vmem((2, 2, COLS, STRIPS * ROWS), F32),
            vmem((2, NX + 2 * PADL, 128), F32),
            vmem((2, 2, NX + 2 * PADX, 128), F32),
            vmem((2, XB, NK, 128), F32),
            vmem((2, XB, NK, 128), F32),
            vmem((2, SUBX, 128), F32),
            vmem((2, 3, 2, SUB, 128), F32),
            vmem((2, 2, SUB, 128), F32),
            vmem((2, 2, 2, SUB, 128), F32),
            vmem((2, 2, SUB, 128), F32),
            dma,
            dma((2,)),
            dma((CHUNKS,)),
            dma((2,)),
            dma((2,)),
            dma((2,)),
            dma((2,)),
            dma((12,)),
            dma((12,)),
        ],
        compiler_params=pltpu.CompilerParams(
            collective_id=0, has_side_effects=True, vmem_limit_bytes=VMEM
        ),
        name="adjoint",
    )(image_grad, jnp.swapaxes(source_field, 1, 2), jnp.swapaxes(receiver_field, 1, 2))
    out = jax.ShapeDtypeStruct((2, ROWS, OUTX), F32)
    return pl.pallas_call(
        turned,
        out_shape=(out, out),
        in_specs=[pl.BlockSpec(memory_space=pltpu.VMEM)],
        out_specs=[pl.BlockSpec(memory_space=pltpu.VMEM)] * 2,
        compiler_params=pltpu.CompilerParams(vmem_limit_bytes=4 << 20),
        name="turned",
    )(result)


def solution(mesh):
    in_specs = (P("lag", "strip", None), P(None, None, "strip"), P(None, None, "strip"))
    out_specs = (P(None, "strip", "lag"), P(None, "strip", "lag"))
    return jax.shard_map(local, mesh=mesh, in_specs=in_specs, out_specs=out_specs, check_vma=False)
```

```python
import jax
import jax.numpy as jnp
from jax import lax
from jax.experimental import pallas as pl
from jax.experimental.pallas import tpu as pltpu
from jax.sharding import PartitionSpec as P

MESH = pl.DeviceIdType.MESH
F32 = jnp.float32

STRIPS = 64
LAGS = 4
NK = 32
PAIRS = NK // 2
ROWS = 64
NX = 1024
XB = NX // 128
COLS = NX // STRIPS
PADD = 16
PIECE = COLS // 2
PHASES = ((1, 0), (1, 1), (0, 0), (0, 1))
PADX = 136
PADF = 72
SLOT = 80
OUTX = NX // LAGS
SUB = 128
HALF = SUB // 2
SUBX = SUB + 8
EXP = 80
VMEM = 56000000
CHUNKS = 4
KC = NK // CHUNKS


def copy_bytes(ref, sem):
    return pltpu.make_async_copy(ref, ref, sem)


def kernel(
    grad, source, receiver, result,
    edge, tiles, smooth, columns, filt, packed, raw, land, twice, field, halo_out, halo_in,
    sums, part, relay, near_in, own,
    edge_sem, raw_sem, load_sem, a2a_send, a2a_recv,
    halo_send, halo_recv, rs_send, rs_recv,
):
    me = lax.axis_index("strip")
    lag = lax.axis_index("lag")
    up_lag = lax.rem(lag + 1, LAGS)
    down_lag = lax.rem(lag + LAGS - 1, LAGS)
    next_strip = lax.rem(me + 1, STRIPS)
    prev_strip = lax.rem(me + STRIPS - 1, STRIPS)
    chip, my_z, my_core = lax.div(me, 4), lax.rem(lax.div(me, 2), 2), lax.rem(me, 2)

    side = lax.rem(lag + LAGS - 1 + 2 * my_z, LAGS)
    crossing = [jnp.where(my_z == z, lag, side) for z in range(2)]
    sender_lag = [lag, crossing[0], lag, crossing[1]]
    target_lag = [jnp.where(my_core == 1, crossing[e // 2], lag) for e in range(4)]

    def each_peer(lags, act):
        def others(j, carry):
            base = lax.rem(chip + j, STRIPS // 4) * 4
            for e in range(4):
                act(base + e, lags[e])
            return carry

        lax.fori_loop(1, STRIPS // 4, others, 0)
        for e in range(1, 4):
            place = lax.rem(lax.rem(me, 4) + e, 4)
            to = lags[0]
            for n in range(1, 4):
                to = jnp.where(place == n, lags[n], to)
            act(chip * 4 + place, to)

    barrier = pltpu.get_barrier_semaphore()

    def greet(strip, to):
        pl.semaphore_signal(barrier, inc=1, device_id=(strip, to), device_id_type=MESH)

    fields = (source, receiver)
    pltpu.make_async_copy(receiver.at[0], raw.at[0], raw_sem.at[0]).start()
    pltpu.make_async_copy(grad.at[:, 0:8, :], edge.at[0], edge_sem).start()
    pltpu.make_async_copy(grad.at[:, ROWS - 8 : ROWS, :], edge.at[1], edge_sem).start()
    for q, (f, t) in enumerate(PHASES):
        if q:
            pltpu.make_async_copy(fields[f].at[t], raw.at[q], raw_sem.at[q]).start()

    each_peer(sender_lag, greet)
    for other in (up_lag, down_lag):
        greet(me, other)
    for other in (next_strip, prev_strip):
        greet(other, lag)

    by_lag = tiles.reshape(NK, XB, SLOT, 128)
    for c in range(CHUNKS):
        for b in range(XB):
            pltpu.make_async_copy(
                grad.at[c * KC : (c + 1) * KC, :, 128 * b : 128 * (b + 1)],
                by_lag.at[c * KC : (c + 1) * KC, b, 8 : 8 + ROWS, :],
                load_sem.at[c],
            ).start()

    low = lax.broadcasted_iota(jnp.int32, (PIECE, 128), 1) < ROWS

    def pack(q):
        def one(j, carry):
            lanes = pl.ds(pl.multiple_of(128 * j, 128), 128)
            first = raw[q, 0:PIECE, lanes]
            second = raw[q, PIECE:COLS, lanes]
            packed[q, 2 * j] = jnp.where(low, first, pltpu.roll(second, ROWS, 1))
            packed[q, 2 * j + 1] = jnp.where(low, pltpu.roll(first, ROWS, 1), second)
            return carry

        copy_bytes(raw.at[q], raw_sem.at[q]).wait()
        lax.fori_loop(0, STRIPS // 2, one, 0, unroll=8)

    pack(0)

    copy_bytes(edge, edge_sem).wait()
    for n in range(2):
        for b in range(XB):
            halo_out[n, b] = edge[n, :, 7 * n, 128 * b : 128 * (b + 1)]

    here = pl.ds(pl.multiple_of(PIECE * me, 8), PIECE)

    def send_field(q):
        def send(strip, to):
            pltpu.make_async_remote_copy(
                packed.at[q, strip], land.at[q, here, :], a2a_send.at[q], a2a_recv.at[q],
                device_id=(strip, to), device_id_type=MESH,
            ).start()

        each_peer(target_lag, send)

    pl.semaphore_wait(barrier, STRIPS - 1 + 4)

    halo_up = pltpu.make_async_remote_copy(
        halo_out.at[1], halo_in.at[0], halo_send.at[0], halo_recv.at[0],
        device_id=(next_strip, lag), device_id_type=MESH,
    )
    halo_down = pltpu.make_async_remote_copy(
        halo_out.at[0], halo_in.at[1], halo_send.at[1], halo_recv.at[1],
        device_id=(prev_strip, lag), device_id_type=MESH,
    )
    halo_up.start()
    halo_down.start()
    send_field(0)
    pack(1)
    send_field(1)

    for n in range(2):
        rows = pl.ds(n * (PADD + NX), PADD)
        twice[rows, :] = jnp.zeros((PADD, 128), F32)
        rows = pl.ds(n * (PADX + NX), PADX)
        field[rows, :] = jnp.zeros((PADX, 128), F32)
        rows = pl.ds(n * (PADF + PAIRS * NX), PADF)
        filt[rows, :] = jnp.zeros((PADF, 128), F32)

    tile_rows = tiles.reshape(NK * XB * SLOT, 128)
    blank = jnp.zeros((NK * XB, 128), F32)
    for row in (7, 8 + ROWS):
        tile_rows[pl.ds(row, NK * XB, stride=SLOT), :] = blank

    def prepare(p, carry):
        columns[p, 0:8, :] = jnp.zeros((8, 128), F32)
        columns[p, 8 + NX :, :] = jnp.zeros((8, 128), F32)
        for b in range(XB):
            centers = []
            for n in range(2):
                j = (2 * p + n) * XB + b
                center = tiles[j, 8 : 8 + ROWS, :]
                above = tiles[j, 7 : 7 + ROWS, :]
                below = tiles[j, 9 : 9 + ROWS, :]
                smooth[j] = 8.0 * center - (above + below)
                centers.append(center)
            columns[p, 8 + 128 * b : 136 + 128 * b, :] = jnp.concatenate(centers, axis=0).T
        return carry

    for c in range(CHUNKS):
        at = pl.ds(c * KC * XB, KC * XB)
        copy_bytes(tiles.at[at, 8 : 8 + ROWS, :], load_sem.at[c]).wait()
        lax.fori_loop(c * KC // 2, (c + 1) * KC // 2, prepare, 0)

    halo_up.wait()
    halo_down.wait()
    smooth_rows = smooth.reshape(NK * XB * ROWS, 128)
    for b in range(XB):
        first = pl.ds(ROWS * b, NK, stride=ROWS * XB)
        last = pl.ds(ROWS * b + ROWS - 1, NK, stride=ROWS * XB)
        above = jnp.where(me == 0, 0.0, halo_in[0, b])
        below = jnp.where(me == STRIPS - 1, 0.0, halo_in[1, b])
        smooth_rows[first, :] = smooth_rows[first, :] - above
        smooth_rows[last, :] = smooth_rows[last, :] - below

    def turn(p, carry):
        for b in range(XB):
            both = [smooth[(2 * p + n) * XB + b] for n in range(2)]
            sides = columns[p, 7 + 128 * b : 135 + 128 * b, :] + columns[p, 9 + 128 * b : 137 + 128 * b, :]
            base = pl.multiple_of(PADF + p * NX + 128 * b, 8)
            filt[pl.ds(base, 128), :] = jnp.concatenate(both, axis=0).T - sides
        return carry

    lax.fori_loop(0, PAIRS, turn, 0)

    first_lag = lag * NK - NK * LAGS // 2

    def lag_copy(n, src, dst, to):
        return pltpu.make_async_remote_copy(
            src, dst, rs_send.at[n], rs_recv.at[n], device_id=(me, to), device_id_type=MESH
        )

    low_x = lax.broadcasted_iota(jnp.int32, (EXP, 128), 1) < ROWS

    def adjoint(q, between):
        sign = 1 if PHASES[q][0] == 1 else -1
        land[q, here, :] = packed[q, me]
        copy_bytes(packed.at[q, 0 : STRIPS - 1], a2a_recv.at[q]).wait()

        def unfold(s, carry):
            this = land[q, pl.ds(pl.multiple_of(PIECE * s, 8), PIECE), :]
            other = pltpu.roll(this, ROWS, 1)
            at = pl.multiple_of(PADD + COLS * s, 8)
            twice[pl.ds(at, PIECE), :] = jnp.where(low, this, other)
            twice[pl.ds(at + PIECE, PIECE), :] = jnp.where(low, other, this)
            return carry

        lax.fori_loop(0, STRIPS, unfold, 0, unroll=8)

        def expand(i, carry):
            at = pl.multiple_of(PADD - 8 + i * EXP, 8)
            to = pl.ds(pl.multiple_of(PADX - 8 + i * EXP, 8), EXP)
            field[to, :] = jnp.where(low_x, twice[pl.ds(at, EXP), :], twice[pl.ds(at + sign, EXP), :])
            return carry

        lax.fori_loop(0, (NX + 16) // EXP, expand, 0)

        half = lax.broadcasted_iota(jnp.int32, (HALF, 128), 1) < ROWS
        start = 0 if sign == 1 else -8

        def products(block, i, out):
            x = block * OUTX + i * SUB + start

            def step(p, total):
                h = (first_lag + 2 * p) * sign
                g = filt[pl.ds(PADF + p * NX + x + h, SUBX), :]
                return total + g * field[pl.ds(PADX + x + 2 * h, SUBX), :]

            sums[...] = lax.fori_loop(0, PAIRS, step, jnp.zeros((SUBX, 128), F32), unroll=4)
            at = 0 if sign == 1 else 8
            a, b = sums[at : at + HALF], sums[at + HALF : at + SUB]
            at += sign
            c, d = sums[at : at + HALF], sums[at + HALF : at + SUB]
            out[...] = jnp.where(half, a, pltpu.roll(b, ROWS, 1)) + jnp.where(
                half, pltpu.roll(c, ROWS, 1), d
            )

        far = lax.rem(lag + 2, LAGS)
        products(far, 0, part.at[q, 0, 0])
        far_up = lag_copy(6 * q, part.at[q, 0, 0], relay.at[q, 0], up_lag)
        far_up.start()
        products(far, 1, part.at[q, 0, 1])
        far_down = lag_copy(6 * q + 1, part.at[q, 0, 1], relay.at[q, 1], down_lag)
        far_down.start()
        between()
        products(up_lag, 1, part.at[q, 1, 1])
        up_1 = lag_copy(6 * q + 2, part.at[q, 1, 1], near_in.at[q, 0, 1], up_lag)
        up_1.start()
        products(down_lag, 0, part.at[q, 2, 0])
        down_0 = lag_copy(6 * q + 3, part.at[q, 2, 0], near_in.at[q, 1, 0], down_lag)
        down_0.start()
        products(up_lag, 0, part.at[q, 1, 0])
        products(down_lag, 1, part.at[q, 2, 1])
        products(lag, 0, own.at[q, 0])
        products(lag, 1, own.at[q, 1])
        up_0 = lag_copy(6 * q + 4, part.at[q, 1, 0], near_in.at[q, 0, 0], up_lag)
        down_1 = lag_copy(6 * q + 5, part.at[q, 2, 1], near_in.at[q, 1, 1], down_lag)
        return far_up, far_down, up_1, down_0, up_0, down_1

    def pass_on(q, copies):
        far_up, far_down, _, _, up_0, down_1 = copies
        far_up.wait_recv()
        part[q, 1, 0] = part[q, 1, 0] + relay[q, 0]
        up_0.start()
        far_down.wait_recv()
        part[q, 2, 1] = part[q, 2, 1] + relay[q, 1]
        down_1.start()

    def finish(q, copies):
        far_up, far_down, up_1, down_0, up_0, down_1 = copies
        for copy in (up_1, down_0, up_0, down_1):
            copy.wait_recv()
        result[q] = 0.25 * (own[q] + near_in[q, 0] + near_in[q, 1])

    def rest_of_fields():
        for q in (2, 3):
            pack(q)
            send_field(q)

    copies = []
    for q in range(4):
        copies.append(
            adjoint(q, (lambda q=q: pass_on(q - 1, copies[q - 1])) if q else rest_of_fields)
        )
    pass_on(3, copies[3])
    for q in range(4):
        finish(q, copies[q])

    for q in range(4):
        for copy in copies[q]:
            copy.wait_send()
        copy_bytes(packed.at[q, 0 : STRIPS - 1], a2a_send.at[q]).wait()


def turned(result, out_s, out_r):
    for q, (f, t) in enumerate(PHASES):
        out = out_s if f == 1 else out_r
        for b in range(OUTX // SUB):
            block = result[q, b].T
            out[t, :, SUB * b : SUB * (b + 1)] = jnp.concatenate([block[0:ROWS], block[ROWS:]], axis=1)


def local(image_grad, source_field, receiver_field):
    vmem = pltpu.VMEM
    dma = pltpu.SemaphoreType.DMA
    result = pl.pallas_call(
        kernel,
        out_shape=jax.ShapeDtypeStruct((4, OUTX // SUB, HALF, 128), F32),
        in_specs=[pl.BlockSpec(memory_space=pltpu.HBM)] * 3,
        out_specs=pl.BlockSpec(memory_space=pltpu.VMEM),
        scratch_shapes=[
            vmem((2, NK, 8, NX), F32),
            vmem((NK * XB, SLOT, 128), F32),
            vmem((NK * XB, ROWS, 128), F32),
            vmem((PAIRS, NX + 16, 128), F32),
            vmem((PAIRS * NX + 2 * PADF, 128), F32),
            vmem((4, STRIPS, PIECE, 128), F32),
            vmem((4, COLS, STRIPS * ROWS), F32),
            vmem((4, STRIPS * PIECE, 128), F32),
            vmem((NX + 2 * PADD, 128), F32),
            vmem((NX + 2 * PADX, 128), F32),
            vmem((2, XB, NK, 128), F32),
            vmem((2, XB, NK, 128), F32),
            vmem((SUBX, 128), F32),
            vmem((4, 3, 2, HALF, 128), F32),
            vmem((4, 2, HALF, 128), F32),
            vmem((4, 2, 2, HALF, 128), F32),
            vmem((4, 2, HALF, 128), F32),
            dma,
            dma((4,)),
            dma((CHUNKS,)),
            dma((4,)),
            dma((4,)),
            dma((2,)),
            dma((2,)),
            dma((24,)),
            dma((24,)),
        ],
        compiler_params=pltpu.CompilerParams(
            collective_id=0, has_side_effects=True, vmem_limit_bytes=VMEM
        ),
        name="adjoint",
    )(image_grad, jnp.swapaxes(source_field, 1, 2), jnp.swapaxes(receiver_field, 1, 2))
    out = jax.ShapeDtypeStruct((2, ROWS, OUTX), F32)
    return pl.pallas_call(
        turned,
        out_shape=(out, out),
        in_specs=[pl.BlockSpec(memory_space=pltpu.VMEM)],
        out_specs=[pl.BlockSpec(memory_space=pltpu.VMEM)] * 2,
        compiler_params=pltpu.CompilerParams(vmem_limit_bytes=4 << 20),
        name="turned",
    )(result)


def solution(mesh):
    in_specs = (P("lag", "strip", None), P(None, None, "strip"), P(None, None, "strip"))
    out_specs = (P(None, "strip", "lag"), P(None, "strip", "lag"))
    return jax.shard_map(local, mesh=mesh, in_specs=in_specs, out_specs=out_specs, check_vma=False)
```

```python
import jax
import jax.numpy as jnp
from jax import lax
from jax.experimental import pallas as pl
from jax.experimental.pallas import tpu as pltpu
from jax.sharding import PartitionSpec as P

MESH = pl.DeviceIdType.MESH
F32 = jnp.float32

STRIPS = 64
LAGS = 4
NK = 32
PAIRS = NK // 2
ROWS = 64
NX = 1024
XB = NX // 128
COLS = NX // STRIPS
PADD = 16
PIECE = COLS // 2
SENDS = (pl.ds(0, 1), pl.ds(1, 1), pl.ds(2, 2))
PHASES = ((1, 0), (1, 1), (0, 0), (0, 1))
PADX = 136
PADF = 72
SLOT = 80
OUTX = NX // LAGS
SUB = 128
HALF = SUB // 2
SUBX = SUB + 8
EXP = 80
VMEM = 56000000
CHUNKS = 4
KC = NK // CHUNKS


def copy_bytes(ref, sem):
    return pltpu.make_async_copy(ref, ref, sem)


def kernel(
    grad, source, receiver, result,
    edge, tiles, smooth, columns, filt, packed, raw, land, twice, field, halo_out, halo_in,
    sums, part, relay, near_in, own,
    edge_sem, raw_sem, load_sem, a2a_send, a2a_recv,
    halo_send, halo_recv, rs_send, rs_recv,
):
    me = lax.axis_index("strip")
    lag = lax.axis_index("lag")
    up_lag = lax.rem(lag + 1, LAGS)
    down_lag = lax.rem(lag + LAGS - 1, LAGS)
    next_strip = lax.rem(me + 1, STRIPS)
    prev_strip = lax.rem(me + STRIPS - 1, STRIPS)
    chip, my_z, my_core = lax.div(me, 4), lax.rem(lax.div(me, 2), 2), lax.rem(me, 2)

    side = lax.rem(lag + LAGS - 1 + 2 * my_z, LAGS)
    crossing = [jnp.where(my_z == z, lag, side) for z in range(2)]
    sender_lag = [lag, crossing[0], lag, crossing[1]]
    target_lag = [jnp.where(my_core == 1, crossing[e // 2], lag) for e in range(4)]

    def each_peer(lags, act):
        def others(j, carry):
            base = lax.rem(chip + j, STRIPS // 4) * 4
            for e in range(4):
                act(base + e, lags[e])
            return carry

        lax.fori_loop(1, STRIPS // 4, others, 0)
        for e in range(1, 4):
            place = lax.rem(lax.rem(me, 4) + e, 4)
            to = lags[0]
            for n in range(1, 4):
                to = jnp.where(place == n, lags[n], to)
            act(chip * 4 + place, to)

    barrier = pltpu.get_barrier_semaphore()

    def greet(strip, to):
        pl.semaphore_signal(barrier, inc=1, device_id=(strip, to), device_id_type=MESH)

    fields = (source, receiver)
    pltpu.make_async_copy(receiver.at[0], raw.at[0], raw_sem.at[0]).start()
    pltpu.make_async_copy(grad.at[:, 0:8, :], edge.at[0], edge_sem).start()
    pltpu.make_async_copy(grad.at[:, ROWS - 8 : ROWS, :], edge.at[1], edge_sem).start()
    for q, (f, t) in enumerate(PHASES):
        if q:
            pltpu.make_async_copy(fields[f].at[t], raw.at[q], raw_sem.at[q]).start()

    each_peer(sender_lag, greet)
    for other in (up_lag, down_lag):
        greet(me, other)
    for other in (next_strip, prev_strip):
        greet(other, lag)

    by_lag = tiles.reshape(NK, XB, SLOT, 128)
    for c in range(CHUNKS):
        for b in range(XB):
            pltpu.make_async_copy(
                grad.at[c * KC : (c + 1) * KC, :, 128 * b : 128 * (b + 1)],
                by_lag.at[c * KC : (c + 1) * KC, b, 8 : 8 + ROWS, :],
                load_sem.at[c],
            ).start()

    low = lax.broadcasted_iota(jnp.int32, (PIECE, 128), 1) < ROWS

    def pack(q):
        def one(j, carry):
            lanes = pl.ds(pl.multiple_of(128 * j, 128), 128)
            first = raw[q, 0:PIECE, lanes]
            second = raw[q, PIECE:COLS, lanes]
            packed[q, 2 * j] = jnp.where(low, first, pltpu.roll(second, ROWS, 1))
            packed[q, 2 * j + 1] = jnp.where(low, pltpu.roll(first, ROWS, 1), second)
            return carry

        copy_bytes(raw.at[q], raw_sem.at[q]).wait()
        lax.fori_loop(0, STRIPS // 2, one, 0, unroll=8)

    pack(0)

    copy_bytes(edge, edge_sem).wait()
    for n in range(2):
        for b in range(XB):
            halo_out[n, b] = edge[n, :, 7 * n, 128 * b : 128 * (b + 1)]

    here = pl.ds(pl.multiple_of(PIECE * me, 8), PIECE)

    def send_field(at):
        def send(strip, to):
            pltpu.make_async_remote_copy(
                packed.at[at, strip], land.at[at, here, :], a2a_send.at[at.start], a2a_recv.at[at.start],
                device_id=(strip, to), device_id_type=MESH,
            ).start()

        each_peer(target_lag, send)

    pl.semaphore_wait(barrier, STRIPS - 1 + 4)

    halo_up = pltpu.make_async_remote_copy(
        halo_out.at[1], halo_in.at[0], halo_send.at[0], halo_recv.at[0],
        device_id=(next_strip, lag), device_id_type=MESH,
    )
    halo_down = pltpu.make_async_remote_copy(
        halo_out.at[0], halo_in.at[1], halo_send.at[1], halo_recv.at[1],
        device_id=(prev_strip, lag), device_id_type=MESH,
    )
    halo_up.start()
    halo_down.start()
    send_field(SENDS[0])
    pack(1)
    send_field(SENDS[1])

    for n in range(2):
        rows = pl.ds(n * (PADD + NX), PADD)
        twice[rows, :] = jnp.zeros((PADD, 128), F32)
        rows = pl.ds(n * (PADX + NX), PADX)
        field[rows, :] = jnp.zeros((PADX, 128), F32)
        rows = pl.ds(n * (PADF + PAIRS * NX), PADF)
        filt[rows, :] = jnp.zeros((PADF, 128), F32)

    tile_rows = tiles.reshape(NK * XB * SLOT, 128)
    blank = jnp.zeros((NK * XB, 128), F32)
    for row in (7, 8 + ROWS):
        tile_rows[pl.ds(row, NK * XB, stride=SLOT), :] = blank

    def prepare(p, carry):
        columns[p, 0:8, :] = jnp.zeros((8, 128), F32)
        columns[p, 8 + NX :, :] = jnp.zeros((8, 128), F32)
        for b in range(XB):
            centers = []
            for n in range(2):
                j = (2 * p + n) * XB + b
                center = tiles[j, 8 : 8 + ROWS, :]
                above = tiles[j, 7 : 7 + ROWS, :]
                below = tiles[j, 9 : 9 + ROWS, :]
                smooth[j] = 8.0 * center - (above + below)
                centers.append(center)
            columns[p, 8 + 128 * b : 136 + 128 * b, :] = jnp.concatenate(centers, axis=0).T
        return carry

    for c in range(CHUNKS):
        at = pl.ds(c * KC * XB, KC * XB)
        copy_bytes(tiles.at[at, 8 : 8 + ROWS, :], load_sem.at[c]).wait()
        lax.fori_loop(c * KC // 2, (c + 1) * KC // 2, prepare, 0, unroll=2)

    pack(2)
    pack(3)
    send_field(SENDS[2])

    halo_up.wait()
    halo_down.wait()
    smooth_rows = smooth.reshape(NK * XB * ROWS, 128)
    for b in range(XB):
        first = pl.ds(ROWS * b, NK, stride=ROWS * XB)
        last = pl.ds(ROWS * b + ROWS - 1, NK, stride=ROWS * XB)
        above = jnp.where(me == 0, 0.0, halo_in[0, b])
        below = jnp.where(me == STRIPS - 1, 0.0, halo_in[1, b])
        smooth_rows[first, :] = smooth_rows[first, :] - above
        smooth_rows[last, :] = smooth_rows[last, :] - below

    def turn(p, carry):
        for b in range(XB):
            both = [smooth[(2 * p + n) * XB + b] for n in range(2)]
            sides = columns[p, 7 + 128 * b : 135 + 128 * b, :] + columns[p, 9 + 128 * b : 137 + 128 * b, :]
            base = pl.multiple_of(PADF + p * NX + 128 * b, 8)
            filt[pl.ds(base, 128), :] = jnp.concatenate(both, axis=0).T - sides
        return carry

    lax.fori_loop(0, PAIRS, turn, 0, unroll=2)

    first_lag = lag * NK - NK * LAGS // 2

    def lag_copy(n, src, dst, to):
        return pltpu.make_async_remote_copy(
            src, dst, rs_send.at[n], rs_recv.at[n], device_id=(me, to), device_id_type=MESH
        )

    low_x = lax.broadcasted_iota(jnp.int32, (EXP, 128), 1) < ROWS

    def adjoint(q, between):
        sign = 1 if PHASES[q][0] == 1 else -1
        land[q, here, :] = packed[q, me]
        if q < len(SENDS):
            copy_bytes(packed.at[SENDS[q], 0 : STRIPS - 1], a2a_recv.at[q]).wait()

        def unfold(s, carry):
            this = land[q, pl.ds(pl.multiple_of(PIECE * s, 8), PIECE), :]
            other = pltpu.roll(this, ROWS, 1)
            at = pl.multiple_of(PADD + COLS * s, 8)
            twice[pl.ds(at, PIECE), :] = jnp.where(low, this, other)
            twice[pl.ds(at + PIECE, PIECE), :] = jnp.where(low, other, this)
            return carry

        lax.fori_loop(0, STRIPS, unfold, 0, unroll=8)

        def expand(i, carry):
            at = pl.multiple_of(PADD - 8 + i * EXP, 8)
            to = pl.ds(pl.multiple_of(PADX - 8 + i * EXP, 8), EXP)
            field[to, :] = jnp.where(low_x, twice[pl.ds(at, EXP), :], twice[pl.ds(at + sign, EXP), :])
            return carry

        lax.fori_loop(0, (NX + 16) // EXP, expand, 0)

        half = lax.broadcasted_iota(jnp.int32, (HALF, 128), 1) < ROWS
        start = 0 if sign == 1 else -8

        def products(block, i, out):
            x = block * OUTX + i * SUB + start

            def step(p, total):
                h = (first_lag + 2 * p) * sign
                g = filt[pl.ds(PADF + p * NX + x + h, SUBX), :]
                return total + g * field[pl.ds(PADX + x + 2 * h, SUBX), :]

            sums[...] = lax.fori_loop(0, PAIRS, step, jnp.zeros((SUBX, 128), F32), unroll=4)
            at = 0 if sign == 1 else 8
            a, b = sums[at : at + HALF], sums[at + HALF : at + SUB]
            at += sign
            c, d = sums[at : at + HALF], sums[at + HALF : at + SUB]
            out[...] = jnp.where(half, a, pltpu.roll(b, ROWS, 1)) + jnp.where(
                half, pltpu.roll(c, ROWS, 1), d
            )

        far = lax.rem(lag + 2, LAGS)
        products(far, 0, part.at[q, 0, 0])
        far_up = lag_copy(6 * q, part.at[q, 0, 0], relay.at[q, 0], up_lag)
        far_up.start()
        products(far, 1, part.at[q, 0, 1])
        far_down = lag_copy(6 * q + 1, part.at[q, 0, 1], relay.at[q, 1], down_lag)
        far_down.start()
        between()
        products(up_lag, 1, part.at[q, 1, 1])
        up_1 = lag_copy(6 * q + 2, part.at[q, 1, 1], near_in.at[q, 0, 1], up_lag)
        up_1.start()
        products(down_lag, 0, part.at[q, 2, 0])
        down_0 = lag_copy(6 * q + 3, part.at[q, 2, 0], near_in.at[q, 1, 0], down_lag)
        down_0.start()
        products(up_lag, 0, part.at[q, 1, 0])
        products(down_lag, 1, part.at[q, 2, 1])
        products(lag, 0, own.at[q, 0])
        products(lag, 1, own.at[q, 1])
        up_0 = lag_copy(6 * q + 4, part.at[q, 1, 0], near_in.at[q, 0, 0], up_lag)
        down_1 = lag_copy(6 * q + 5, part.at[q, 2, 1], near_in.at[q, 1, 1], down_lag)
        return far_up, far_down, up_1, down_0, up_0, down_1

    def pass_on(q, copies):
        far_up, far_down, _, _, up_0, down_1 = copies
        far_up.wait_recv()
        part[q, 1, 0] = part[q, 1, 0] + relay[q, 0]
        up_0.start()
        far_down.wait_recv()
        part[q, 2, 1] = part[q, 2, 1] + relay[q, 1]
        down_1.start()

    def finish(q, copies):
        far_up, far_down, up_1, down_0, up_0, down_1 = copies
        for copy in (up_1, down_0, up_0, down_1):
            copy.wait_recv()
        result[q] = 0.25 * (own[q] + near_in[q, 0] + near_in[q, 1])

    copies = []
    for q in range(4):
        copies.append(
            adjoint(q, (lambda q=q: pass_on(q - 1, copies[q - 1])) if q else lambda: None)
        )
    pass_on(3, copies[3])
    for q in range(4):
        finish(q, copies[q])

    for q in range(4):
        for copy in copies[q]:
            copy.wait_send()
    for n, at in enumerate(SENDS):
        copy_bytes(packed.at[at, 0 : STRIPS - 1], a2a_send.at[n]).wait()


def turned(result, out_s, out_r):
    for q, (f, t) in enumerate(PHASES):
        out = out_s if f == 1 else out_r
        for b in range(OUTX // SUB):
            block = result[q, b].T
            out[t, :, SUB * b : SUB * (b + 1)] = jnp.concatenate([block[0:ROWS], block[ROWS:]], axis=1)


def local(image_grad, source_field, receiver_field):
    vmem = pltpu.VMEM
    dma = pltpu.SemaphoreType.DMA
    result = pl.pallas_call(
        kernel,
        out_shape=jax.ShapeDtypeStruct((4, OUTX // SUB, HALF, 128), F32),
        in_specs=[pl.BlockSpec(memory_space=pltpu.HBM)] * 3,
        out_specs=pl.BlockSpec(memory_space=pltpu.VMEM),
        scratch_shapes=[
            vmem((2, NK, 8, NX), F32),
            vmem((NK * XB, SLOT, 128), F32),
            vmem((NK * XB, ROWS, 128), F32),
            vmem((PAIRS, NX + 16, 128), F32),
            vmem((PAIRS * NX + 2 * PADF, 128), F32),
            vmem((4, STRIPS, PIECE, 128), F32),
            vmem((4, COLS, STRIPS * ROWS), F32),
            vmem((4, STRIPS * PIECE, 128), F32),
            vmem((NX + 2 * PADD, 128), F32),
            vmem((NX + 2 * PADX, 128), F32),
            vmem((2, XB, NK, 128), F32),
            vmem((2, XB, NK, 128), F32),
            vmem((SUBX, 128), F32),
            vmem((4, 3, 2, HALF, 128), F32),
            vmem((4, 2, HALF, 128), F32),
            vmem((4, 2, 2, HALF, 128), F32),
            vmem((4, 2, HALF, 128), F32),
            dma,
            dma((4,)),
            dma((CHUNKS,)),
            dma((3,)),
            dma((3,)),
            dma((2,)),
            dma((2,)),
            dma((24,)),
            dma((24,)),
        ],
        compiler_params=pltpu.CompilerParams(
            collective_id=0, has_side_effects=True, vmem_limit_bytes=VMEM
        ),
        name="adjoint",
    )(image_grad, jnp.swapaxes(source_field, 1, 2), jnp.swapaxes(receiver_field, 1, 2))
    out = jax.ShapeDtypeStruct((2, ROWS, OUTX), F32)
    return pl.pallas_call(
        turned,
        out_shape=(out, out),
        in_specs=[pl.BlockSpec(memory_space=pltpu.VMEM)],
        out_specs=[pl.BlockSpec(memory_space=pltpu.VMEM)] * 2,
        compiler_params=pltpu.CompilerParams(vmem_limit_bytes=4 << 20),
        name="turned",
    )(result)


def solution(mesh):
    in_specs = (P("lag", "strip", None), P(None, None, "strip"), P(None, None, "strip"))
    out_specs = (P(None, "strip", "lag"), P(None, "strip", "lag"))
    return jax.shard_map(local, mesh=mesh, in_specs=in_specs, out_specs=out_specs, check_vma=False)
```

```python
import jax
import jax.numpy as jnp
from jax import lax
from jax.experimental import pallas as pl
from jax.experimental.pallas import tpu as pltpu
from jax.sharding import PartitionSpec as P

MESH = pl.DeviceIdType.MESH
F32 = jnp.float32

STRIPS = 64
LAGS = 4
NK = 32
PAIRS = NK // 2
ROWS = 64
NX = 1024
XB = NX // 128
COLS = NX // STRIPS
PADD = 16
PIECE = COLS // 2
SENDS = (pl.ds(0, 1), pl.ds(1, 1), pl.ds(2, 2))
PHASES = ((1, 0), (1, 1), (0, 0), (0, 1))
PADX = 136
PADF = 72
SLOT = 80
OUTX = NX // LAGS
SUB = 128
HALF = SUB // 2
SUBX = SUB + 8
EXP = 80
VMEM = 56000000
EARLY = 2
CHUNKS = 4
KC = NK // CHUNKS


def copy_bytes(ref, sem):
    return pltpu.make_async_copy(ref, ref, sem)


def kernel(
    grad, source, receiver, result,
    edge, tiles, smooth, columns, filt, packed, raw, land, twice, field, halo_out, halo_in,
    sums, part, relay, near_in, own,
    edge_sem, raw_sem, load_sem, a2a_send, a2a_recv,
    halo_send, halo_recv, rs_send, rs_recv,
):
    me = lax.axis_index("strip")
    lag = lax.axis_index("lag")
    up_lag = lax.rem(lag + 1, LAGS)
    down_lag = lax.rem(lag + LAGS - 1, LAGS)
    next_strip = lax.rem(me + 1, STRIPS)
    prev_strip = lax.rem(me + STRIPS - 1, STRIPS)
    chip, my_z, my_core = lax.div(me, 4), lax.rem(lax.div(me, 2), 2), lax.rem(me, 2)

    side = lax.rem(lag + LAGS - 1 + 2 * my_z, LAGS)
    crossing = [jnp.where(my_z == z, lag, side) for z in range(2)]
    sender_lag = [lag, crossing[0], lag, crossing[1]]
    target_lag = [jnp.where(my_core == 1, crossing[e // 2], lag) for e in range(4)]

    def each_peer(lags, act):
        def others(j, carry):
            base = lax.rem(chip + j, STRIPS // 4) * 4
            for e in range(4):
                act(base + e, lags[e])
            return carry

        lax.fori_loop(1, STRIPS // 4, others, 0)
        for e in range(1, 4):
            place = lax.rem(lax.rem(me, 4) + e, 4)
            to = lags[0]
            for n in range(1, 4):
                to = jnp.where(place == n, lags[n], to)
            act(chip * 4 + place, to)

    barrier = pltpu.get_barrier_semaphore()

    def greet(strip, to):
        pl.semaphore_signal(barrier, inc=1, device_id=(strip, to), device_id_type=MESH)

    fields = (source, receiver)
    pltpu.make_async_copy(receiver.at[0], raw.at[0], raw_sem.at[0]).start()
    pltpu.make_async_copy(grad.at[:, 0:8, :], edge.at[0], edge_sem).start()
    pltpu.make_async_copy(grad.at[:, ROWS - 8 : ROWS, :], edge.at[1], edge_sem).start()
    for q, (f, t) in enumerate(PHASES):
        if q:
            pltpu.make_async_copy(fields[f].at[t], raw.at[q], raw_sem.at[q]).start()

    each_peer(sender_lag, greet)
    for other in (up_lag, down_lag):
        greet(me, other)
    for other in (next_strip, prev_strip):
        greet(other, lag)

    by_lag = tiles.reshape(NK, XB, SLOT, 128)
    for c in range(CHUNKS):
        for b in range(XB):
            pltpu.make_async_copy(
                grad.at[c * KC : (c + 1) * KC, :, 128 * b : 128 * (b + 1)],
                by_lag.at[c * KC : (c + 1) * KC, b, 8 : 8 + ROWS, :],
                load_sem.at[c],
            ).start()

    low = lax.broadcasted_iota(jnp.int32, (PIECE, 128), 1) < ROWS

    def pack(q):
        def one(j, carry):
            lanes = pl.ds(pl.multiple_of(128 * j, 128), 128)
            first = raw[q, 0:PIECE, lanes]
            second = raw[q, PIECE:COLS, lanes]
            packed[q, 2 * j] = jnp.where(low, first, pltpu.roll(second, ROWS, 1))
            packed[q, 2 * j + 1] = jnp.where(low, pltpu.roll(first, ROWS, 1), second)
            return carry

        copy_bytes(raw.at[q], raw_sem.at[q]).wait()
        lax.fori_loop(0, STRIPS // 2, one, 0, unroll=8)

    pack(0)

    copy_bytes(edge, edge_sem).wait()
    for n in range(2):
        for b in range(XB):
            halo_out[n, b] = edge[n, :, 7 * n, 128 * b : 128 * (b + 1)]

    here = pl.ds(pl.multiple_of(PIECE * me, 8), PIECE)

    def send_field(at):
        def send(strip, to):
            pltpu.make_async_remote_copy(
                packed.at[at, strip], land.at[at, here, :], a2a_send.at[at.start], a2a_recv.at[at.start],
                device_id=(strip, to), device_id_type=MESH,
            ).start()

        each_peer(target_lag, send)

    for q in range(1, 4):
        pack(q)

    for n in range(2):
        rows = pl.ds(n * (PADD + NX), PADD)
        twice[rows, :] = jnp.zeros((PADD, 128), F32)
        rows = pl.ds(n * (PADX + NX), PADX)
        field[rows, :] = jnp.zeros((PADX, 128), F32)
        rows = pl.ds(n * (PADF + PAIRS * NX), PADF)
        filt[rows, :] = jnp.zeros((PADF, 128), F32)

    tile_rows = tiles.reshape(NK * XB * SLOT, 128)
    blank = jnp.zeros((NK * XB, 128), F32)
    for row in (7, 8 + ROWS):
        tile_rows[pl.ds(row, NK * XB, stride=SLOT), :] = blank

    def prepare(p, carry):
        columns[p, 0:8, :] = jnp.zeros((8, 128), F32)
        columns[p, 8 + NX :, :] = jnp.zeros((8, 128), F32)
        for b in range(XB):
            centers = []
            for n in range(2):
                j = (2 * p + n) * XB + b
                center = tiles[j, 8 : 8 + ROWS, :]
                above = tiles[j, 7 : 7 + ROWS, :]
                below = tiles[j, 9 : 9 + ROWS, :]
                smooth[j] = 8.0 * center - (above + below)
                centers.append(center)
            columns[p, 8 + 128 * b : 136 + 128 * b, :] = jnp.concatenate(centers, axis=0).T
        return carry

    def prepare_chunk(c):
        at = pl.ds(c * KC * XB, KC * XB)
        copy_bytes(tiles.at[at, 8 : 8 + ROWS, :], load_sem.at[c]).wait()
        lax.fori_loop(c * KC // 2, (c + 1) * KC // 2, prepare, 0, unroll=2)

    for c in range(EARLY):
        prepare_chunk(c)

    pl.semaphore_wait(barrier, STRIPS - 1 + 4)

    halo_up = pltpu.make_async_remote_copy(
        halo_out.at[1], halo_in.at[0], halo_send.at[0], halo_recv.at[0],
        device_id=(next_strip, lag), device_id_type=MESH,
    )
    halo_down = pltpu.make_async_remote_copy(
        halo_out.at[0], halo_in.at[1], halo_send.at[1], halo_recv.at[1],
        device_id=(prev_strip, lag), device_id_type=MESH,
    )
    halo_up.start()
    halo_down.start()
    for at in SENDS:
        send_field(at)

    for c in range(EARLY, CHUNKS):
        prepare_chunk(c)

    halo_up.wait()
    halo_down.wait()
    smooth_rows = smooth.reshape(NK * XB * ROWS, 128)
    for b in range(XB):
        first = pl.ds(ROWS * b, NK, stride=ROWS * XB)
        last = pl.ds(ROWS * b + ROWS - 1, NK, stride=ROWS * XB)
        above = jnp.where(me == 0, 0.0, halo_in[0, b])
        below = jnp.where(me == STRIPS - 1, 0.0, halo_in[1, b])
        smooth_rows[first, :] = smooth_rows[first, :] - above
        smooth_rows[last, :] = smooth_rows[last, :] - below

    def turn(p, carry):
        for b in range(XB):
            both = [smooth[(2 * p + n) * XB + b] for n in range(2)]
            sides = columns[p, 7 + 128 * b : 135 + 128 * b, :] + columns[p, 9 + 128 * b : 137 + 128 * b, :]
            base = pl.multiple_of(PADF + p * NX + 128 * b, 8)
            filt[pl.ds(base, 128), :] = jnp.concatenate(both, axis=0).T - sides
        return carry

    lax.fori_loop(0, PAIRS, turn, 0, unroll=2)

    first_lag = lag * NK - NK * LAGS // 2

    def lag_copy(n, src, dst, to):
        return pltpu.make_async_remote_copy(
            src, dst, rs_send.at[n], rs_recv.at[n], device_id=(me, to), device_id_type=MESH
        )

    low_x = lax.broadcasted_iota(jnp.int32, (EXP, 128), 1) < ROWS

    def adjoint(q, between):
        sign = 1 if PHASES[q][0] == 1 else -1
        land[q, here, :] = packed[q, me]
        if q < len(SENDS):
            copy_bytes(packed.at[SENDS[q], 0 : STRIPS - 1], a2a_recv.at[q]).wait()

        def unfold(s, carry):
            this = land[q, pl.ds(pl.multiple_of(PIECE * s, 8), PIECE), :]
            other = pltpu.roll(this, ROWS, 1)
            at = pl.multiple_of(PADD + COLS * s, 8)
            twice[pl.ds(at, PIECE), :] = jnp.where(low, this, other)
            twice[pl.ds(at + PIECE, PIECE), :] = jnp.where(low, other, this)
            return carry

        lax.fori_loop(0, STRIPS, unfold, 0, unroll=8)

        def expand(i, carry):
            at = pl.multiple_of(PADD - 8 + i * EXP, 8)
            to = pl.ds(pl.multiple_of(PADX - 8 + i * EXP, 8), EXP)
            field[to, :] = jnp.where(low_x, twice[pl.ds(at, EXP), :], twice[pl.ds(at + sign, EXP), :])
            return carry

        lax.fori_loop(0, (NX + 16) // EXP, expand, 0)

        half = lax.broadcasted_iota(jnp.int32, (HALF, 128), 1) < ROWS
        start = 0 if sign == 1 else -8

        def products(block, i, out):
            x = block * OUTX + i * SUB + start

            def step(p, total):
                h = (first_lag + 2 * p) * sign
                g = filt[pl.ds(PADF + p * NX + x + h, SUBX), :]
                return total + g * field[pl.ds(PADX + x + 2 * h, SUBX), :]

            sums[...] = lax.fori_loop(0, PAIRS, step, jnp.zeros((SUBX, 128), F32), unroll=4)
            at = 0 if sign == 1 else 8
            a, b = sums[at : at + HALF], sums[at + HALF : at + SUB]
            at += sign
            c, d = sums[at : at + HALF], sums[at + HALF : at + SUB]
            out[...] = jnp.where(half, a, pltpu.roll(b, ROWS, 1)) + jnp.where(
                half, pltpu.roll(c, ROWS, 1), d
            )

        far = lax.rem(lag + 2, LAGS)
        products(far, 0, part.at[q, 0, 0])
        far_up = lag_copy(6 * q, part.at[q, 0, 0], relay.at[q, 0], up_lag)
        far_up.start()
        products(far, 1, part.at[q, 0, 1])
        far_down = lag_copy(6 * q + 1, part.at[q, 0, 1], relay.at[q, 1], down_lag)
        far_down.start()
        between()
        products(up_lag, 1, part.at[q, 1, 1])
        up_1 = lag_copy(6 * q + 2, part.at[q, 1, 1], near_in.at[q, 0, 1], up_lag)
        up_1.start()
        products(down_lag, 0, part.at[q, 2, 0])
        down_0 = lag_copy(6 * q + 3, part.at[q, 2, 0], near_in.at[q, 1, 0], down_lag)
        down_0.start()
        products(up_lag, 0, part.at[q, 1, 0])
        products(down_lag, 1, part.at[q, 2, 1])
        products(lag, 0, own.at[q, 0])
        products(lag, 1, own.at[q, 1])
        up_0 = lag_copy(6 * q + 4, part.at[q, 1, 0], near_in.at[q, 0, 0], up_lag)
        down_1 = lag_copy(6 * q + 5, part.at[q, 2, 1], near_in.at[q, 1, 1], down_lag)
        return far_up, far_down, up_1, down_0, up_0, down_1

    def pass_on(q, copies):
        far_up, far_down, _, _, up_0, down_1 = copies
        far_up.wait_recv()
        part[q, 1, 0] = part[q, 1, 0] + relay[q, 0]
        up_0.start()
        far_down.wait_recv()
        part[q, 2, 1] = part[q, 2, 1] + relay[q, 1]
        down_1.start()

    def finish(q, copies):
        far_up, far_down, up_1, down_0, up_0, down_1 = copies
        for copy in (up_1, down_0, up_0, down_1):
            copy.wait_recv()
        result[q] = 0.25 * (own[q] + near_in[q, 0] + near_in[q, 1])

    copies = []
    for q in range(4):
        copies.append(
            adjoint(q, (lambda q=q: pass_on(q - 1, copies[q - 1])) if q else lambda: None)
        )
    pass_on(3, copies[3])
    for q in range(4):
        finish(q, copies[q])

    for q in range(4):
        for copy in copies[q]:
            copy.wait_send()
    for n, at in enumerate(SENDS):
        copy_bytes(packed.at[at, 0 : STRIPS - 1], a2a_send.at[n]).wait()


def turned(result, out_s, out_r):
    for q, (f, t) in enumerate(PHASES):
        out = out_s if f == 1 else out_r
        for b in range(OUTX // SUB):
            block = result[q, b].T
            out[t, :, SUB * b : SUB * (b + 1)] = jnp.concatenate([block[0:ROWS], block[ROWS:]], axis=1)


def local(image_grad, source_field, receiver_field):
    vmem = pltpu.VMEM
    dma = pltpu.SemaphoreType.DMA
    result = pl.pallas_call(
        kernel,
        out_shape=jax.ShapeDtypeStruct((4, OUTX // SUB, HALF, 128), F32),
        in_specs=[pl.BlockSpec(memory_space=pltpu.HBM)] * 3,
        out_specs=pl.BlockSpec(memory_space=pltpu.VMEM),
        scratch_shapes=[
            vmem((2, NK, 8, NX), F32),
            vmem((NK * XB, SLOT, 128), F32),
            vmem((NK * XB, ROWS, 128), F32),
            vmem((PAIRS, NX + 16, 128), F32),
            vmem((PAIRS * NX + 2 * PADF, 128), F32),
            vmem((4, STRIPS, PIECE, 128), F32),
            vmem((4, COLS, STRIPS * ROWS), F32),
            vmem((4, STRIPS * PIECE, 128), F32),
            vmem((NX + 2 * PADD, 128), F32),
            vmem((NX + 2 * PADX, 128), F32),
            vmem((2, XB, NK, 128), F32),
            vmem((2, XB, NK, 128), F32),
            vmem((SUBX, 128), F32),
            vmem((4, 3, 2, HALF, 128), F32),
            vmem((4, 2, HALF, 128), F32),
            vmem((4, 2, 2, HALF, 128), F32),
            vmem((4, 2, HALF, 128), F32),
            dma,
            dma((4,)),
            dma((CHUNKS,)),
            dma((3,)),
            dma((3,)),
            dma((2,)),
            dma((2,)),
            dma((24,)),
            dma((24,)),
        ],
        compiler_params=pltpu.CompilerParams(
            collective_id=0, has_side_effects=True, vmem_limit_bytes=VMEM
        ),
        name="adjoint",
    )(image_grad, jnp.swapaxes(source_field, 1, 2), jnp.swapaxes(receiver_field, 1, 2))
    out = jax.ShapeDtypeStruct((2, ROWS, OUTX), F32)
    return pl.pallas_call(
        turned,
        out_shape=(out, out),
        in_specs=[pl.BlockSpec(memory_space=pltpu.VMEM)],
        out_specs=[pl.BlockSpec(memory_space=pltpu.VMEM)] * 2,
        compiler_params=pltpu.CompilerParams(vmem_limit_bytes=4 << 20),
        name="turned",
    )(result)


def solution(mesh):
    in_specs = (P("lag", "strip", None), P(None, None, "strip"), P(None, None, "strip"))
    out_specs = (P(None, "strip", "lag"), P(None, "strip", "lag"))
    return jax.shard_map(local, mesh=mesh, in_specs=in_specs, out_specs=out_specs, check_vma=False)
```

```python
import jax
import jax.numpy as jnp
from jax import lax
from jax.experimental import pallas as pl
from jax.experimental.pallas import tpu as pltpu
from jax.sharding import PartitionSpec as P

MESH = pl.DeviceIdType.MESH
F32 = jnp.float32

STRIPS = 64
LAGS = 4
NK = 32
PAIRS = NK // 2
ROWS = 64
NX = 1024
XB = NX // 128
COLS = NX // STRIPS
PADD = 16
PIECE = COLS // 2
SENDS = (pl.ds(0, 1), pl.ds(1, 1), pl.ds(2, 2))
PHASES = ((1, 0), (1, 1), (0, 0), (0, 1))
PADX = 136
PADF = 72
SLOT = 80
OUTX = NX // LAGS
SUB = 128
HALF = SUB // 2
SUBX = SUB + 8
EXP = 80
VMEM = 56000000
CHUNKS = 4
KC = NK // CHUNKS


def copy_bytes(ref, sem):
    return pltpu.make_async_copy(ref, ref, sem)


def kernel(
    grad, source, receiver, result,
    edge, tiles, smooth, columns, filt, packed, raw, land, twice, field, halo_out, halo_in,
    sums, part, relay, near_in, own,
    edge_sem, raw_sem, load_sem, a2a_send, a2a_recv,
    halo_send, halo_recv, rs_send, rs_recv,
):
    me = lax.axis_index("strip")
    lag = lax.axis_index("lag")
    up_lag = lax.rem(lag + 1, LAGS)
    down_lag = lax.rem(lag + LAGS - 1, LAGS)
    next_strip = lax.rem(me + 1, STRIPS)
    prev_strip = lax.rem(me + STRIPS - 1, STRIPS)
    chip, my_z, my_core = lax.div(me, 4), lax.rem(lax.div(me, 2), 2), lax.rem(me, 2)

    side = lax.rem(lag + LAGS - 1 + 2 * my_z, LAGS)
    crossing = [jnp.where(my_z == z, lag, side) for z in range(2)]
    sender_lag = [lag, crossing[0], lag, crossing[1]]
    target_lag = [jnp.where(my_core == 1, crossing[e // 2], lag) for e in range(4)]

    def each_peer(lags, act):
        def others(j, carry):
            base = lax.rem(chip + j, STRIPS // 4) * 4
            for e in range(4):
                act(base + e, lags[e])
            return carry

        lax.fori_loop(1, STRIPS // 4, others, 0)
        for e in range(1, 4):
            place = lax.rem(lax.rem(me, 4) + e, 4)
            to = lags[0]
            for n in range(1, 4):
                to = jnp.where(place == n, lags[n], to)
            act(chip * 4 + place, to)

    barrier = pltpu.get_barrier_semaphore()

    def greet(strip, to):
        pl.semaphore_signal(barrier, inc=1, device_id=(strip, to), device_id_type=MESH)

    fields = (source, receiver)
    pltpu.make_async_copy(receiver.at[0], raw.at[0], raw_sem.at[0]).start()
    pltpu.make_async_copy(grad.at[:, 0:8, :], edge.at[0], edge_sem).start()
    pltpu.make_async_copy(grad.at[:, ROWS - 8 : ROWS, :], edge.at[1], edge_sem).start()
    for q, (f, t) in enumerate(PHASES):
        if q:
            pltpu.make_async_copy(fields[f].at[t], raw.at[q], raw_sem.at[q]).start()

    each_peer(sender_lag, greet)
    for other in (up_lag, down_lag):
        greet(me, other)
    for other in (next_strip, prev_strip):
        greet(other, lag)

    by_lag = tiles.reshape(NK, XB, SLOT, 128)
    for c in range(CHUNKS):
        for b in range(XB):
            pltpu.make_async_copy(
                grad.at[c * KC : (c + 1) * KC, :, 128 * b : 128 * (b + 1)],
                by_lag.at[c * KC : (c + 1) * KC, b, 8 : 8 + ROWS, :],
                load_sem.at[c],
            ).start()

    low = lax.broadcasted_iota(jnp.int32, (PIECE, 128), 1) < ROWS

    def pack(q):
        def one(j, carry):
            lanes = pl.ds(pl.multiple_of(128 * j, 128), 128)
            first = raw[q, 0:PIECE, lanes]
            second = raw[q, PIECE:COLS, lanes]
            packed[q, 2 * j] = jnp.where(low, first, pltpu.roll(second, ROWS, 1))
            packed[q, 2 * j + 1] = jnp.where(low, pltpu.roll(first, ROWS, 1), second)
            return carry

        copy_bytes(raw.at[q], raw_sem.at[q]).wait()
        lax.fori_loop(0, STRIPS // 2, one, 0, unroll=8)

    tile_rows = tiles.reshape(NK * XB * SLOT, 128)
    for row in (7, 8 + ROWS):
        tile_rows[pl.ds(row, NK * XB, stride=SLOT), :] = jnp.zeros((NK * XB, 128), F32)
    for n in range(2):
        rows = pl.ds(n * (PADD + NX), PADD)
        twice[rows, :] = jnp.zeros((PADD, 128), F32)
        rows = pl.ds(n * (PADX + NX), PADX)
        field[rows, :] = jnp.zeros((PADX, 128), F32)
        rows = pl.ds(n * (PADF + PAIRS * NX), PADF)
        filt[rows, :] = jnp.zeros((PADF, 128), F32)

    pack(0)

    copy_bytes(edge, edge_sem).wait()
    for n in range(2):
        for b in range(XB):
            halo_out[n, b] = edge[n, :, 7 * n, 128 * b : 128 * (b + 1)]

    here = pl.ds(pl.multiple_of(PIECE * me, 8), PIECE)

    def send_field(at):
        def send(strip, to):
            pltpu.make_async_remote_copy(
                packed.at[at, strip], land.at[at, here, :], a2a_send.at[at.start], a2a_recv.at[at.start],
                device_id=(strip, to), device_id_type=MESH,
            ).start()

        each_peer(target_lag, send)

    pl.semaphore_wait(barrier, STRIPS - 1 + 4)

    halo_up = pltpu.make_async_remote_copy(
        halo_out.at[1], halo_in.at[0], halo_send.at[0], halo_recv.at[0],
        device_id=(next_strip, lag), device_id_type=MESH,
    )
    halo_down = pltpu.make_async_remote_copy(
        halo_out.at[0], halo_in.at[1], halo_send.at[1], halo_recv.at[1],
        device_id=(prev_strip, lag), device_id_type=MESH,
    )
    send_field(SENDS[0])
    halo_up.start()
    halo_down.start()
    pack(1)
    send_field(SENDS[1])

    def prepare(p, carry):
        columns[p, 0:8, :] = jnp.zeros((8, 128), F32)
        columns[p, 8 + NX :, :] = jnp.zeros((8, 128), F32)
        for b in range(XB):
            centers = []
            for n in range(2):
                j = (2 * p + n) * XB + b
                center = tiles[j, 8 : 8 + ROWS, :]
                above = tiles[j, 7 : 7 + ROWS, :]
                below = tiles[j, 9 : 9 + ROWS, :]
                smooth[j] = 8.0 * center - (above + below)
                centers.append(center)
            columns[p, 8 + 128 * b : 136 + 128 * b, :] = jnp.concatenate(centers, axis=0).T
        return carry

    for c in range(CHUNKS):
        at = pl.ds(c * KC * XB, KC * XB)
        copy_bytes(tiles.at[at, 8 : 8 + ROWS, :], load_sem.at[c]).wait()
        lax.fori_loop(c * KC // 2, (c + 1) * KC // 2, prepare, 0, unroll=2)

    pack(2)
    pack(3)
    send_field(SENDS[2])

    halo_up.wait()
    halo_down.wait()
    halo_in[0] = jnp.where(me == 0, 0.0, halo_in[0])
    halo_in[1] = jnp.where(me == STRIPS - 1, 0.0, halo_in[1])
    top = lax.broadcasted_iota(jnp.int32, (8, 128), 0) == 0
    bottom = lax.broadcasted_iota(jnp.int32, (8, 128), 0) == 7
    far = lax.rem(lag + 2, LAGS)

    def turn(blocks):
        at = [lax.rem(2 * far + XB - 1 + n, XB) for n in blocks]

        def one(p, carry):
            for b in at:
                parts = []
                for n in range(2):
                    k = 2 * p + n
                    j = k * XB + b
                    above = jnp.broadcast_to(halo_in[0, b, pl.ds(k, 1), :], (8, 128))
                    below = jnp.broadcast_to(halo_in[1, b, pl.ds(k, 1), :], (8, 128))
                    first, last = smooth[j, 0:8, :], smooth[j, ROWS - 8 : ROWS, :]
                    parts += [
                        jnp.where(top, first - above, first),
                        smooth[j, 8 : ROWS - 8, :],
                        jnp.where(bottom, last - below, last),
                    ]
                x = 128 * b
                sides = columns[p, pl.ds(x + 7, 128), :] + columns[p, pl.ds(x + 9, 128), :]
                base = pl.multiple_of(PADF + p * NX + x, 8)
                filt[pl.ds(base, 128), :] = jnp.concatenate(parts, axis=0).T - sides
            return carry

        lax.fori_loop(0, PAIRS, one, 0, unroll=4)

    turn(range(0, 4))

    first_lag = lag * NK - NK * LAGS // 2

    def lag_copy(n, src, dst, to):
        return pltpu.make_async_remote_copy(
            src, dst, rs_send.at[n], rs_recv.at[n], device_id=(me, to), device_id_type=MESH
        )

    low_x = lax.broadcasted_iota(jnp.int32, (EXP, 128), 1) < ROWS

    def adjoint(q, between):
        sign = 1 if PHASES[q][0] == 1 else -1
        land[q, here, :] = packed[q, me]
        if q < len(SENDS):
            copy_bytes(packed.at[SENDS[q], 0 : STRIPS - 1], a2a_recv.at[q]).wait()

        def unfold(s, carry):
            this = land[q, pl.ds(pl.multiple_of(PIECE * s, 8), PIECE), :]
            other = pltpu.roll(this, ROWS, 1)
            at = pl.multiple_of(PADD + COLS * s, 8)
            twice[pl.ds(at, PIECE), :] = jnp.where(low, this, other)
            twice[pl.ds(at + PIECE, PIECE), :] = jnp.where(low, other, this)
            return carry

        lax.fori_loop(0, STRIPS, unfold, 0, unroll=8)

        def expand(i, carry):
            at = pl.multiple_of(PADD - 8 + i * EXP, 8)
            to = pl.ds(pl.multiple_of(PADX - 8 + i * EXP, 8), EXP)
            field[to, :] = jnp.where(low_x, twice[pl.ds(at, EXP), :], twice[pl.ds(at + sign, EXP), :])
            return carry

        lax.fori_loop(0, (NX + 16) // EXP, expand, 0)

        half = lax.broadcasted_iota(jnp.int32, (HALF, 128), 1) < ROWS
        start = 0 if sign == 1 else -8

        def products(block, i, out):
            x = block * OUTX + i * SUB + start

            def step(p, total):
                h = (first_lag + 2 * p) * sign
                g = filt[pl.ds(PADF + p * NX + x + h, SUBX), :]
                return total + g * field[pl.ds(PADX + x + 2 * h, SUBX), :]

            sums[...] = lax.fori_loop(0, PAIRS, step, jnp.zeros((SUBX, 128), F32), unroll=4)
            at = 0 if sign == 1 else 8
            a, b = sums[at : at + HALF], sums[at + HALF : at + SUB]
            at += sign
            c, d = sums[at : at + HALF], sums[at + HALF : at + SUB]
            out[...] = jnp.where(half, a, pltpu.roll(b, ROWS, 1)) + jnp.where(
                half, pltpu.roll(c, ROWS, 1), d
            )

        products(far, 0, part.at[q, 0, 0])
        far_up = lag_copy(6 * q, part.at[q, 0, 0], relay.at[q, 0], up_lag)
        far_up.start()
        products(far, 1, part.at[q, 0, 1])
        far_down = lag_copy(6 * q + 1, part.at[q, 0, 1], relay.at[q, 1], down_lag)
        far_down.start()
        between()
        products(up_lag, 1, part.at[q, 1, 1])
        up_1 = lag_copy(6 * q + 2, part.at[q, 1, 1], near_in.at[q, 0, 1], up_lag)
        up_1.start()
        products(down_lag, 0, part.at[q, 2, 0])
        down_0 = lag_copy(6 * q + 3, part.at[q, 2, 0], near_in.at[q, 1, 0], down_lag)
        down_0.start()
        products(up_lag, 0, part.at[q, 1, 0])
        products(down_lag, 1, part.at[q, 2, 1])
        products(lag, 0, own.at[q, 0])
        products(lag, 1, own.at[q, 1])
        up_0 = lag_copy(6 * q + 4, part.at[q, 1, 0], near_in.at[q, 0, 0], up_lag)
        down_1 = lag_copy(6 * q + 5, part.at[q, 2, 1], near_in.at[q, 1, 1], down_lag)
        return far_up, far_down, up_1, down_0, up_0, down_1

    def pass_on(q, copies):
        far_up, far_down, _, _, up_0, down_1 = copies
        far_up.wait_recv()
        part[q, 1, 0] = part[q, 1, 0] + relay[q, 0]
        up_0.start()
        far_down.wait_recv()
        part[q, 2, 1] = part[q, 2, 1] + relay[q, 1]
        down_1.start()

    def finish(q, copies):
        far_up, far_down, up_1, down_0, up_0, down_1 = copies
        for copy in (up_1, down_0, up_0, down_1):
            copy.wait_recv()
        result[q] = 0.25 * (own[q] + near_in[q, 0] + near_in[q, 1])

    copies = []
    for q in range(4):
        copies.append(
            adjoint(q, (lambda q=q: pass_on(q - 1, copies[q - 1])) if q else lambda: turn(range(4, 8)))
        )
    pass_on(3, copies[3])
    for q in range(4):
        finish(q, copies[q])

    for q in range(4):
        for copy in copies[q]:
            copy.wait_send()
    for n, at in enumerate(SENDS):
        copy_bytes(packed.at[at, 0 : STRIPS - 1], a2a_send.at[n]).wait()


def turned(result, out_s, out_r):
    for q, (f, t) in enumerate(PHASES):
        out = out_s if f == 1 else out_r
        for b in range(OUTX // SUB):
            block = result[q, b].T
            out[t, :, SUB * b : SUB * (b + 1)] = jnp.concatenate([block[0:ROWS], block[ROWS:]], axis=1)


def local(image_grad, source_field, receiver_field):
    vmem = pltpu.VMEM
    dma = pltpu.SemaphoreType.DMA
    result = pl.pallas_call(
        kernel,
        out_shape=jax.ShapeDtypeStruct((4, OUTX // SUB, HALF, 128), F32),
        in_specs=[pl.BlockSpec(memory_space=pltpu.HBM)] * 3,
        out_specs=pl.BlockSpec(memory_space=pltpu.VMEM),
        scratch_shapes=[
            vmem((2, NK, 8, NX), F32),
            vmem((NK * XB, SLOT, 128), F32),
            vmem((NK * XB, ROWS, 128), F32),
            vmem((PAIRS, NX + 16, 128), F32),
            vmem((PAIRS * NX + 2 * PADF, 128), F32),
            vmem((4, STRIPS, PIECE, 128), F32),
            vmem((4, COLS, STRIPS * ROWS), F32),
            vmem((4, STRIPS * PIECE, 128), F32),
            vmem((NX + 2 * PADD, 128), F32),
            vmem((NX + 2 * PADX, 128), F32),
            vmem((2, XB, NK, 128), F32),
            vmem((2, XB, NK, 128), F32),
            vmem((SUBX, 128), F32),
            vmem((4, 3, 2, HALF, 128), F32),
            vmem((4, 2, HALF, 128), F32),
            vmem((4, 2, 2, HALF, 128), F32),
            vmem((4, 2, HALF, 128), F32),
            dma,
            dma((4,)),
            dma((CHUNKS,)),
            dma((3,)),
            dma((3,)),
            dma((2,)),
            dma((2,)),
            dma((24,)),
            dma((24,)),
        ],
        compiler_params=pltpu.CompilerParams(
            collective_id=0, has_side_effects=True, vmem_limit_bytes=VMEM
        ),
        name="adjoint",
    )(image_grad, jnp.swapaxes(source_field, 1, 2), jnp.swapaxes(receiver_field, 1, 2))
    out = jax.ShapeDtypeStruct((2, ROWS, OUTX), F32)
    return pl.pallas_call(
        turned,
        out_shape=(out, out),
        in_specs=[pl.BlockSpec(memory_space=pltpu.VMEM)],
        out_specs=[pl.BlockSpec(memory_space=pltpu.VMEM)] * 2,
        compiler_params=pltpu.CompilerParams(vmem_limit_bytes=4 << 20),
        name="turned",
    )(result)


def solution(mesh):
    in_specs = (P("lag", "strip", None), P(None, None, "strip"), P(None, None, "strip"))
    out_specs = (P(None, "strip", "lag"), P(None, "strip", "lag"))
    return jax.shard_map(local, mesh=mesh, in_specs=in_specs, out_specs=out_specs, check_vma=False)
```

```python
import jax
import jax.numpy as jnp
from jax import lax
from jax.experimental import pallas as pl
from jax.experimental.pallas import tpu as pltpu
from jax.sharding import PartitionSpec as P

MESH = pl.DeviceIdType.MESH
F32 = jnp.float32

STRIPS = 64
LAGS = 4
NK = 32
PAIRS = NK // 2
ROWS = 64
NX = 1024
XB = NX // 128
COLS = NX // STRIPS
PADD = 16
PIECE = COLS // 2
SENDS = (pl.ds(0, 1), pl.ds(1, 1), pl.ds(2, 2))
PHASES = ((1, 0), (1, 1), (0, 0), (0, 1))
PADX = 136
PADF = 72
SLOT = 80
OUTX = NX // LAGS
SUB = 128
HALF = SUB // 2
SUBX = SUB + 8
EXP = 80
VMEM = 56000000
CHUNKS = 4
KC = NK // CHUNKS


def copy_bytes(ref, sem):
    return pltpu.make_async_copy(ref, ref, sem)


def kernel(
    grad, source, receiver, result,
    edge, tiles, smooth, columns, filt, packed, raw, land, twice, field, halo_out, halo_in,
    sums, part, relay, near_in, own,
    edge_sem, raw_sem, load_sem, a2a_send, a2a_recv,
    halo_send, halo_recv, rs_send, rs_recv,
):
    me = lax.axis_index("strip")
    lag = lax.axis_index("lag")
    up_lag = lax.rem(lag + 1, LAGS)
    down_lag = lax.rem(lag + LAGS - 1, LAGS)
    next_strip = lax.rem(me + 1, STRIPS)
    prev_strip = lax.rem(me + STRIPS - 1, STRIPS)
    chip, my_z, my_core = lax.div(me, 4), lax.rem(lax.div(me, 2), 2), lax.rem(me, 2)

    side = lax.rem(lag + LAGS - 1 + 2 * my_z, LAGS)
    crossing = [jnp.where(my_z == z, lag, side) for z in range(2)]
    sender_lag = [lag, crossing[0], lag, crossing[1]]
    target_lag = [jnp.where(my_core == 1, crossing[e // 2], lag) for e in range(4)]

    def each_peer(lags, act):
        def others(j, carry):
            base = lax.rem(chip + j, STRIPS // 4) * 4
            for e in range(4):
                act(base + e, lags[e])
            return carry

        lax.fori_loop(1, STRIPS // 4, others, 0)
        for e in range(1, 4):
            place = lax.rem(lax.rem(me, 4) + e, 4)
            to = lags[0]
            for n in range(1, 4):
                to = jnp.where(place == n, lags[n], to)
            act(chip * 4 + place, to)

    barrier = pltpu.get_barrier_semaphore()

    def greet(strip, to):
        pl.semaphore_signal(barrier, inc=1, device_id=(strip, to), device_id_type=MESH)

    fields = (source, receiver)
    pltpu.make_async_copy(receiver.at[0], raw.at[0], raw_sem.at[0]).start()
    pltpu.make_async_copy(grad.at[:, 0:8, :], edge.at[0], edge_sem).start()
    pltpu.make_async_copy(grad.at[:, ROWS - 8 : ROWS, :], edge.at[1], edge_sem).start()
    for q, (f, t) in enumerate(PHASES):
        if q:
            pltpu.make_async_copy(fields[f].at[t], raw.at[q], raw_sem.at[q]).start()

    each_peer(sender_lag, greet)
    for other in (up_lag, down_lag):
        greet(me, other)
    for other in (next_strip, prev_strip):
        greet(other, lag)

    by_lag = tiles.reshape(NK, XB, SLOT, 128)
    for c in range(CHUNKS):
        for b in range(XB):
            pltpu.make_async_copy(
                grad.at[c * KC : (c + 1) * KC, :, 128 * b : 128 * (b + 1)],
                by_lag.at[c * KC : (c + 1) * KC, b, 8 : 8 + ROWS, :],
                load_sem.at[c],
            ).start()

    low = lax.broadcasted_iota(jnp.int32, (PIECE, 128), 1) < ROWS

    def pack(q):
        def one(j, carry):
            lanes = pl.ds(pl.multiple_of(128 * j, 128), 128)
            first = raw[q, 0:PIECE, lanes]
            second = raw[q, PIECE:COLS, lanes]
            packed[q, 2 * j] = jnp.where(low, first, pltpu.roll(second, ROWS, 1))
            packed[q, 2 * j + 1] = jnp.where(low, pltpu.roll(first, ROWS, 1), second)
            return carry

        copy_bytes(raw.at[q], raw_sem.at[q]).wait()
        lax.fori_loop(0, STRIPS // 2, one, 0, unroll=8)

    pack(0)

    copy_bytes(edge, edge_sem).wait()
    for n in range(2):
        for b in range(XB):
            halo_out[n, b] = edge[n, :, 7 * n, 128 * b : 128 * (b + 1)]

    here = pl.ds(pl.multiple_of(PIECE * me, 8), PIECE)

    def send_field(at):
        def send(strip, to):
            pltpu.make_async_remote_copy(
                packed.at[at, strip], land.at[at, here, :], a2a_send.at[at.start], a2a_recv.at[at.start],
                device_id=(strip, to), device_id_type=MESH,
            ).start()

        each_peer(target_lag, send)

    pl.semaphore_wait(barrier, STRIPS - 1 + 4)

    halo_up = pltpu.make_async_remote_copy(
        halo_out.at[1], halo_in.at[0], halo_send.at[0], halo_recv.at[0],
        device_id=(next_strip, lag), device_id_type=MESH,
    )
    halo_down = pltpu.make_async_remote_copy(
        halo_out.at[0], halo_in.at[1], halo_send.at[1], halo_recv.at[1],
        device_id=(prev_strip, lag), device_id_type=MESH,
    )
    halo_up.start()
    halo_down.start()
    send_field(SENDS[0])
    pack(1)
    send_field(SENDS[1])

    for n in range(2):
        rows = pl.ds(n * (PADD + NX), PADD)
        twice[rows, :] = jnp.zeros((PADD, 128), F32)
        rows = pl.ds(n * (PADX + NX), PADX)
        for m in range(2):
            field[m, rows, :] = jnp.zeros((PADX, 128), F32)
        rows = pl.ds(n * (PADF + PAIRS * NX), PADF)
        filt[rows, :] = jnp.zeros((PADF, 128), F32)

    tile_rows = tiles.reshape(NK * XB * SLOT, 128)
    blank = jnp.zeros((NK * XB, 128), F32)
    for row in (7, 8 + ROWS):
        tile_rows[pl.ds(row, NK * XB, stride=SLOT), :] = blank

    def prepare(p, carry):
        columns[p, 0:8, :] = jnp.zeros((8, 128), F32)
        columns[p, 8 + NX :, :] = jnp.zeros((8, 128), F32)
        for b in range(XB):
            centers = []
            for n in range(2):
                j = (2 * p + n) * XB + b
                center = tiles[j, 8 : 8 + ROWS, :]
                above = tiles[j, 7 : 7 + ROWS, :]
                below = tiles[j, 9 : 9 + ROWS, :]
                smooth[j] = 8.0 * center - (above + below)
                centers.append(center)
            columns[p, 8 + 128 * b : 136 + 128 * b, :] = jnp.concatenate(centers, axis=0).T
        return carry

    for c in range(CHUNKS):
        at = pl.ds(c * KC * XB, KC * XB)
        copy_bytes(tiles.at[at, 8 : 8 + ROWS, :], load_sem.at[c]).wait()
        lax.fori_loop(c * KC // 2, (c + 1) * KC // 2, prepare, 0, unroll=2)

    pack(2)
    pack(3)
    send_field(SENDS[2])

    halo_up.wait()
    halo_down.wait()
    smooth_rows = smooth.reshape(NK * XB * ROWS, 128)
    for b in range(XB):
        first = pl.ds(ROWS * b, NK, stride=ROWS * XB)
        last = pl.ds(ROWS * b + ROWS - 1, NK, stride=ROWS * XB)
        above = jnp.where(me == 0, 0.0, halo_in[0, b])
        below = jnp.where(me == STRIPS - 1, 0.0, halo_in[1, b])
        smooth_rows[first, :] = smooth_rows[first, :] - above
        smooth_rows[last, :] = smooth_rows[last, :] - below

    def turn(p, carry):
        for b in range(XB):
            both = [smooth[(2 * p + n) * XB + b] for n in range(2)]
            sides = columns[p, 7 + 128 * b : 135 + 128 * b, :] + columns[p, 9 + 128 * b : 137 + 128 * b, :]
            base = pl.multiple_of(PADF + p * NX + 128 * b, 8)
            filt[pl.ds(base, 128), :] = jnp.concatenate(both, axis=0).T - sides
        return carry

    lax.fori_loop(0, PAIRS, turn, 0, unroll=2)

    first_lag = lag * NK - NK * LAGS // 2

    def lag_copy(n, src, dst, to):
        return pltpu.make_async_remote_copy(
            src, dst, rs_send.at[n], rs_recv.at[n], device_id=(me, to), device_id_type=MESH
        )

    low_x = lax.broadcasted_iota(jnp.int32, (EXP, 128), 1) < ROWS

    def sign_of(q):
        return 1 if PHASES[q][0] == 1 else -1

    def arrive(q):
        sign = sign_of(q)
        land[q, here, :] = packed[q, me]
        if q < len(SENDS):
            copy_bytes(packed.at[SENDS[q], 0 : STRIPS - 1], a2a_recv.at[q]).wait()

        def unfold(s, carry):
            this = land[q, pl.ds(pl.multiple_of(PIECE * s, 8), PIECE), :]
            other = pltpu.roll(this, ROWS, 1)
            at = pl.multiple_of(PADD + COLS * s, 8)
            twice[pl.ds(at, PIECE), :] = jnp.where(low, this, other)
            twice[pl.ds(at + PIECE, PIECE), :] = jnp.where(low, other, this)
            return carry

        lax.fori_loop(0, STRIPS, unfold, 0, unroll=8)

        def expand(i, carry):
            at = pl.multiple_of(PADD - 8 + i * EXP, 8)
            to = pl.ds(pl.multiple_of(PADX - 8 + i * EXP, 8), EXP)
            field[q % 2, to, :] = jnp.where(low_x, twice[pl.ds(at, EXP), :], twice[pl.ds(at + sign, EXP), :])
            return carry

        lax.fori_loop(0, (NX + 16) // EXP, expand, 0)

    half = lax.broadcasted_iota(jnp.int32, (HALF, 128), 1) < ROWS

    def products(q, block, i, out):
        sign = sign_of(q)
        x = block * OUTX + i * SUB + (0 if sign == 1 else -8)

        def step(p, total):
            h = (first_lag + 2 * p) * sign
            g = filt[pl.ds(PADF + p * NX + x + h, SUBX), :]
            return total + g * field[q % 2, pl.ds(PADX + x + 2 * h, SUBX), :]

        sums[...] = lax.fori_loop(0, PAIRS, step, jnp.zeros((SUBX, 128), F32), unroll=4)
        at = 0 if sign == 1 else 8
        a, b = sums[at : at + HALF], sums[at + HALF : at + SUB]
        at += sign
        c, d = sums[at : at + HALF], sums[at + HALF : at + SUB]
        out[...] = jnp.where(half, a, pltpu.roll(b, ROWS, 1)) + jnp.where(
            half, pltpu.roll(c, ROWS, 1), d
        )

    far_lag = lax.rem(lag + 2, LAGS)

    def copies_of(q):
        far_up = lag_copy(6 * q, part.at[q, 0, 0], relay.at[q, 0], up_lag)
        far_down = lag_copy(6 * q + 1, part.at[q, 0, 1], relay.at[q, 1], down_lag)
        up_1 = lag_copy(6 * q + 2, part.at[q, 1, 1], near_in.at[q, 0, 1], up_lag)
        down_0 = lag_copy(6 * q + 3, part.at[q, 2, 0], near_in.at[q, 1, 0], down_lag)
        up_0 = lag_copy(6 * q + 4, part.at[q, 1, 0], near_in.at[q, 0, 0], up_lag)
        down_1 = lag_copy(6 * q + 5, part.at[q, 2, 1], near_in.at[q, 1, 1], down_lag)
        return far_up, far_down, up_1, down_0, up_0, down_1

    copies = [copies_of(q) for q in range(4)]

    def far(q):
        arrive(q)
        products(q, far_lag, 0, part.at[q, 0, 0])
        copies[q][0].start()
        products(q, far_lag, 1, part.at[q, 0, 1])
        copies[q][1].start()

    def direct(q):
        products(q, up_lag, 1, part.at[q, 1, 1])
        copies[q][2].start()
        products(q, down_lag, 0, part.at[q, 2, 0])
        copies[q][3].start()

    def joined(q):
        products(q, up_lag, 0, part.at[q, 1, 0])
        products(q, down_lag, 1, part.at[q, 2, 1])
        products(q, lag, 0, own.at[q, 0])
        products(q, lag, 1, own.at[q, 1])

    def pass_on(q):
        far_up, far_down, _, _, up_0, down_1 = copies[q]
        far_up.wait_recv()
        part[q, 1, 0] = part[q, 1, 0] + relay[q, 0]
        up_0.start()
        far_down.wait_recv()
        part[q, 2, 1] = part[q, 2, 1] + relay[q, 1]
        down_1.start()

    def finish(q):
        for copy in copies[q][2:]:
            copy.wait_recv()
        result[q] = 0.25 * (own[q] + near_in[q, 0] + near_in[q, 1])

    for first in (0, 2):
        pair = (first, first + 1)
        for q in pair:
            far(q)
        if first:
            pass_on(0)
            pass_on(1)
        for q in pair:
            direct(q)
        for q in pair:
            joined(q)
    pass_on(2)
    pass_on(3)
    for q in range(4):
        finish(q)

    for q in range(4):
        for copy in copies[q]:
            copy.wait_send()
    for n, at in enumerate(SENDS):
        copy_bytes(packed.at[at, 0 : STRIPS - 1], a2a_send.at[n]).wait()


def turned(result, out_s, out_r):
    for q, (f, t) in enumerate(PHASES):
        out = out_s if f == 1 else out_r
        for b in range(OUTX // SUB):
            block = result[q, b].T
            out[t, :, SUB * b : SUB * (b + 1)] = jnp.concatenate([block[0:ROWS], block[ROWS:]], axis=1)


def local(image_grad, source_field, receiver_field):
    vmem = pltpu.VMEM
    dma = pltpu.SemaphoreType.DMA
    result = pl.pallas_call(
        kernel,
        out_shape=jax.ShapeDtypeStruct((4, OUTX // SUB, HALF, 128), F32),
        in_specs=[pl.BlockSpec(memory_space=pltpu.HBM)] * 3,
        out_specs=pl.BlockSpec(memory_space=pltpu.VMEM),
        scratch_shapes=[
            vmem((2, NK, 8, NX), F32),
            vmem((NK * XB, SLOT, 128), F32),
            vmem((NK * XB, ROWS, 128), F32),
            vmem((PAIRS, NX + 16, 128), F32),
            vmem((PAIRS * NX + 2 * PADF, 128), F32),
            vmem((4, STRIPS, PIECE, 128), F32),
            vmem((4, COLS, STRIPS * ROWS), F32),
            vmem((4, STRIPS * PIECE, 128), F32),
            vmem((NX + 2 * PADD, 128), F32),
            vmem((2, NX + 2 * PADX, 128), F32),
            vmem((2, XB, NK, 128), F32),
            vmem((2, XB, NK, 128), F32),
            vmem((SUBX, 128), F32),
            vmem((4, 3, 2, HALF, 128), F32),
            vmem((4, 2, HALF, 128), F32),
            vmem((4, 2, 2, HALF, 128), F32),
            vmem((4, 2, HALF, 128), F32),
            dma,
            dma((4,)),
            dma((CHUNKS,)),
            dma((3,)),
            dma((3,)),
            dma((2,)),
            dma((2,)),
            dma((24,)),
            dma((24,)),
        ],
        compiler_params=pltpu.CompilerParams(
            collective_id=0, has_side_effects=True, vmem_limit_bytes=VMEM
        ),
        name="adjoint",
    )(image_grad, jnp.swapaxes(source_field, 1, 2), jnp.swapaxes(receiver_field, 1, 2))
    out = jax.ShapeDtypeStruct((2, ROWS, OUTX), F32)
    return pl.pallas_call(
        turned,
        out_shape=(out, out),
        in_specs=[pl.BlockSpec(memory_space=pltpu.VMEM)],
        out_specs=[pl.BlockSpec(memory_space=pltpu.VMEM)] * 2,
        compiler_params=pltpu.CompilerParams(vmem_limit_bytes=4 << 20),
        name="turned",
    )(result)


def solution(mesh):
    in_specs = (P("lag", "strip", None), P(None, None, "strip"), P(None, None, "strip"))
    out_specs = (P(None, "strip", "lag"), P(None, "strip", "lag"))
    return jax.shard_map(local, mesh=mesh, in_specs=in_specs, out_specs=out_specs, check_vma=False)
```

```python
import jax
import jax.numpy as jnp
from jax import lax
from jax.experimental import pallas as pl
from jax.experimental.pallas import tpu as pltpu
from jax.sharding import PartitionSpec as P

MESH = pl.DeviceIdType.MESH
F32 = jnp.float32

STRIPS = 64
LAGS = 4
NK = 32
PAIRS = NK // 2
ROWS = 64
NX = 1024
XB = NX // 128
COLS = NX // STRIPS
PADD = 16
PIECE = COLS // 2
SENDS = (pl.ds(0, 1), pl.ds(1, 1), pl.ds(2, 2))
PHASES = ((1, 0), (1, 1), (0, 0), (0, 1))
PADX = 136
PADF = 72
SLOT = 80
OUTX = NX // LAGS
SUB = 128
HALF = SUB // 2
SUBX = SUB + 8
EXP = 80
VMEM = 56000000
CHUNKS = 4
KC = NK // CHUNKS


def copy_bytes(ref, sem):
    return pltpu.make_async_copy(ref, ref, sem)


def kernel(
    grad, source, receiver, result,
    edge, tiles, smooth, columns, filt, packed, raw, land, twice, field, halo_out, halo_in,
    sums, part, relay, near_in, own,
    edge_sem, raw_sem, load_sem, a2a_send, a2a_recv,
    halo_send, halo_recv, rs_send, rs_recv,
):
    me = lax.axis_index("strip")
    lag = lax.axis_index("lag")
    up_lag = lax.rem(lag + 1, LAGS)
    down_lag = lax.rem(lag + LAGS - 1, LAGS)
    next_strip = lax.rem(me + 1, STRIPS)
    prev_strip = lax.rem(me + STRIPS - 1, STRIPS)
    chip, my_z, my_core = lax.div(me, 4), lax.rem(lax.div(me, 2), 2), lax.rem(me, 2)

    side = lax.rem(lag + LAGS - 1 + 2 * my_z, LAGS)
    crossing = [jnp.where(my_z == z, lag, side) for z in range(2)]
    sender_lag = [lag, crossing[0], lag, crossing[1]]
    target_lag = [jnp.where(my_core == 1, crossing[e // 2], lag) for e in range(4)]

    def each_peer(lags, act):
        def others(j, carry):
            base = lax.rem(chip + j, STRIPS // 4) * 4
            for e in range(4):
                act(base + e, lags[e])
            return carry

        lax.fori_loop(1, STRIPS // 4, others, 0)
        for e in range(1, 4):
            place = lax.rem(lax.rem(me, 4) + e, 4)
            to = lags[0]
            for n in range(1, 4):
                to = jnp.where(place == n, lags[n], to)
            act(chip * 4 + place, to)

    barrier = pltpu.get_barrier_semaphore()

    def greet(strip, to):
        pl.semaphore_signal(barrier, inc=1, device_id=(strip, to), device_id_type=MESH)

    fields = (source, receiver)
    pltpu.make_async_copy(receiver.at[0], raw.at[0], raw_sem.at[0]).start()
    pltpu.make_async_copy(grad.at[:, 0:8, :], edge.at[0], edge_sem).start()
    pltpu.make_async_copy(grad.at[:, ROWS - 8 : ROWS, :], edge.at[1], edge_sem).start()
    for q, (f, t) in enumerate(PHASES):
        if q:
            pltpu.make_async_copy(fields[f].at[t], raw.at[q], raw_sem.at[q]).start()

    each_peer(sender_lag, greet)
    for other in (up_lag, down_lag):
        greet(me, other)
    for other in (next_strip, prev_strip):
        greet(other, lag)

    by_lag = tiles.reshape(NK, XB, SLOT, 128)
    for c in range(CHUNKS):
        for b in range(XB):
            pltpu.make_async_copy(
                grad.at[c * KC : (c + 1) * KC, :, 128 * b : 128 * (b + 1)],
                by_lag.at[c * KC : (c + 1) * KC, b, 8 : 8 + ROWS, :],
                load_sem.at[c],
            ).start()

    low = lax.broadcasted_iota(jnp.int32, (PIECE, 128), 1) < ROWS

    def pack(q):
        def one(j, carry):
            lanes = pl.ds(pl.multiple_of(128 * j, 128), 128)
            first = raw[q, 0:PIECE, lanes]
            second = raw[q, PIECE:COLS, lanes]
            packed[q, 2 * j] = jnp.where(low, first, pltpu.roll(second, ROWS, 1))
            packed[q, 2 * j + 1] = jnp.where(low, pltpu.roll(first, ROWS, 1), second)
            return carry

        copy_bytes(raw.at[q], raw_sem.at[q]).wait()
        lax.fori_loop(0, STRIPS // 2, one, 0, unroll=8)

    tile_rows = tiles.reshape(NK * XB * SLOT, 128)
    for row in (7, 8 + ROWS):
        tile_rows[pl.ds(row, NK * XB, stride=SLOT), :] = jnp.zeros((NK * XB, 128), F32)
    for n in range(2):
        rows = pl.ds(n * (PADD + NX), PADD)
        twice[rows, :] = jnp.zeros((PADD, 128), F32)
        rows = pl.ds(n * (PADX + NX), PADX)
        for m in range(2):
            field[m, rows, :] = jnp.zeros((PADX, 128), F32)
        rows = pl.ds(n * (PADF + PAIRS * NX), PADF)
        filt[rows, :] = jnp.zeros((PADF, 128), F32)

    pack(0)

    copy_bytes(edge, edge_sem).wait()
    for n in range(2):
        for b in range(XB):
            halo_out[n, b] = edge[n, :, 7 * n, 128 * b : 128 * (b + 1)]

    here = pl.ds(pl.multiple_of(PIECE * me, 8), PIECE)

    def send_field(at):
        def send(strip, to):
            pltpu.make_async_remote_copy(
                packed.at[at, strip], land.at[at, here, :], a2a_send.at[at.start], a2a_recv.at[at.start],
                device_id=(strip, to), device_id_type=MESH,
            ).start()

        each_peer(target_lag, send)

    pl.semaphore_wait(barrier, STRIPS - 1 + 4)

    halo_up = pltpu.make_async_remote_copy(
        halo_out.at[1], halo_in.at[0], halo_send.at[0], halo_recv.at[0],
        device_id=(next_strip, lag), device_id_type=MESH,
    )
    halo_down = pltpu.make_async_remote_copy(
        halo_out.at[0], halo_in.at[1], halo_send.at[1], halo_recv.at[1],
        device_id=(prev_strip, lag), device_id_type=MESH,
    )
    halo_up.start()
    halo_down.start()
    send_field(SENDS[0])
    pack(1)
    send_field(SENDS[1])

    def prepare(p, carry):
        columns[p, 0:8, :] = jnp.zeros((8, 128), F32)
        columns[p, 8 + NX :, :] = jnp.zeros((8, 128), F32)
        for b in range(XB):
            centers = []
            for n in range(2):
                j = (2 * p + n) * XB + b
                center = tiles[j, 8 : 8 + ROWS, :]
                above = tiles[j, 7 : 7 + ROWS, :]
                below = tiles[j, 9 : 9 + ROWS, :]
                smooth[j] = 8.0 * center - (above + below)
                centers.append(center)
            columns[p, 8 + 128 * b : 136 + 128 * b, :] = jnp.concatenate(centers, axis=0).T
        return carry

    for c in range(CHUNKS):
        at = pl.ds(c * KC * XB, KC * XB)
        copy_bytes(tiles.at[at, 8 : 8 + ROWS, :], load_sem.at[c]).wait()
        lax.fori_loop(c * KC // 2, (c + 1) * KC // 2, prepare, 0, unroll=2)

    pack(2)
    pack(3)
    send_field(SENDS[2])

    halo_up.wait()
    halo_down.wait()
    halo_in[0] = jnp.where(me == 0, 0.0, halo_in[0])
    halo_in[1] = jnp.where(me == STRIPS - 1, 0.0, halo_in[1])
    top = lax.broadcasted_iota(jnp.int32, (8, 128), 0) == 0
    bottom = lax.broadcasted_iota(jnp.int32, (8, 128), 0) == 7
    far_lag = lax.rem(lag + 2, LAGS)

    def turn(blocks):
        at = [lax.rem(2 * far_lag + XB - 1 + n, XB) for n in blocks]

        def one(p, carry):
            for b in at:
                parts = []
                for n in range(2):
                    k = 2 * p + n
                    j = k * XB + b
                    above = jnp.broadcast_to(halo_in[0, b, pl.ds(k, 1), :], (8, 128))
                    below = jnp.broadcast_to(halo_in[1, b, pl.ds(k, 1), :], (8, 128))
                    first, last = smooth[j, 0:8, :], smooth[j, ROWS - 8 : ROWS, :]
                    parts += [
                        jnp.where(top, first - above, first),
                        smooth[j, 8 : ROWS - 8, :],
                        jnp.where(bottom, last - below, last),
                    ]
                x = 128 * b
                sides = columns[p, pl.ds(x + 7, 128), :] + columns[p, pl.ds(x + 9, 128), :]
                base = pl.multiple_of(PADF + p * NX + x, 8)
                filt[pl.ds(base, 128), :] = jnp.concatenate(parts, axis=0).T - sides
            return carry

        lax.fori_loop(0, PAIRS, one, 0, unroll=2)

    turn(range(XB))

    first_lag = lag * NK - NK * LAGS // 2

    def lag_copy(n, src, dst, to):
        return pltpu.make_async_remote_copy(
            src, dst, rs_send.at[n], rs_recv.at[n], device_id=(me, to), device_id_type=MESH
        )

    low_x = lax.broadcasted_iota(jnp.int32, (EXP, 128), 1) < ROWS

    def sign_of(q):
        return 1 if PHASES[q][0] == 1 else -1

    def arrive(q):
        sign = sign_of(q)
        land[q, here, :] = packed[q, me]
        if q < len(SENDS):
            copy_bytes(packed.at[SENDS[q], 0 : STRIPS - 1], a2a_recv.at[q]).wait()

        def unfold(s, carry):
            this = land[q, pl.ds(pl.multiple_of(PIECE * s, 8), PIECE), :]
            other = pltpu.roll(this, ROWS, 1)
            at = pl.multiple_of(PADD + COLS * s, 8)
            twice[pl.ds(at, PIECE), :] = jnp.where(low, this, other)
            twice[pl.ds(at + PIECE, PIECE), :] = jnp.where(low, other, this)
            return carry

        lax.fori_loop(0, STRIPS, unfold, 0, unroll=8)

        def expand(i, carry):
            at = pl.multiple_of(PADD - 8 + i * EXP, 8)
            to = pl.ds(pl.multiple_of(PADX - 8 + i * EXP, 8), EXP)
            field[q % 2, to, :] = jnp.where(low_x, twice[pl.ds(at, EXP), :], twice[pl.ds(at + sign, EXP), :])
            return carry

        lax.fori_loop(0, (NX + 16) // EXP, expand, 0)

    half = lax.broadcasted_iota(jnp.int32, (HALF, 128), 1) < ROWS

    def products(q, block, i, out):
        sign = sign_of(q)
        x = block * OUTX + i * SUB + (0 if sign == 1 else -8)

        def step(p, total):
            h = (first_lag + 2 * p) * sign
            g = filt[pl.ds(PADF + p * NX + x + h, SUBX), :]
            return total + g * field[q % 2, pl.ds(PADX + x + 2 * h, SUBX), :]

        sums[...] = lax.fori_loop(0, PAIRS, step, jnp.zeros((SUBX, 128), F32), unroll=4)
        at = 0 if sign == 1 else 8
        a, b = sums[at : at + HALF], sums[at + HALF : at + SUB]
        at += sign
        c, d = sums[at : at + HALF], sums[at + HALF : at + SUB]
        out[...] = jnp.where(half, a, pltpu.roll(b, ROWS, 1)) + jnp.where(
            half, pltpu.roll(c, ROWS, 1), d
        )

    def copies_of(q):
        far_up = lag_copy(6 * q, part.at[q, 0, 0], relay.at[q, 0], up_lag)
        far_down = lag_copy(6 * q + 1, part.at[q, 0, 1], relay.at[q, 1], down_lag)
        up_1 = lag_copy(6 * q + 2, part.at[q, 1, 1], near_in.at[q, 0, 1], up_lag)
        down_0 = lag_copy(6 * q + 3, part.at[q, 2, 0], near_in.at[q, 1, 0], down_lag)
        up_0 = lag_copy(6 * q + 4, part.at[q, 1, 0], near_in.at[q, 0, 0], up_lag)
        down_1 = lag_copy(6 * q + 5, part.at[q, 2, 1], near_in.at[q, 1, 1], down_lag)
        return far_up, far_down, up_1, down_0, up_0, down_1

    copies = [copies_of(q) for q in range(4)]

    def far(q):
        arrive(q)
        products(q, far_lag, 0, part.at[q, 0, 0])
        copies[q][0].start()
        products(q, far_lag, 1, part.at[q, 0, 1])
        copies[q][1].start()

    def direct(q):
        products(q, up_lag, 1, part.at[q, 1, 1])
        copies[q][2].start()
        products(q, down_lag, 0, part.at[q, 2, 0])
        copies[q][3].start()

    def joined(q):
        products(q, up_lag, 0, part.at[q, 1, 0])
        products(q, down_lag, 1, part.at[q, 2, 1])
        products(q, lag, 0, own.at[q, 0])
        products(q, lag, 1, own.at[q, 1])

    def pass_on(q):
        far_up, far_down, _, _, up_0, down_1 = copies[q]
        far_up.wait_recv()
        part[q, 1, 0] = part[q, 1, 0] + relay[q, 0]
        up_0.start()
        far_down.wait_recv()
        part[q, 2, 1] = part[q, 2, 1] + relay[q, 1]
        down_1.start()

    def finish(q):
        for copy in copies[q][2:]:
            copy.wait_recv()
        result[q] = 0.25 * (own[q] + near_in[q, 0] + near_in[q, 1])

    for first in (0, 2):
        pair = (first, first + 1)
        for q in pair:
            far(q)
        if first:
            pass_on(0)
            pass_on(1)
        for q in pair:
            direct(q)
        for q in pair:
            joined(q)
    pass_on(2)
    pass_on(3)
    for q in range(4):
        finish(q)

    for q in range(4):
        for copy in copies[q]:
            copy.wait_send()
    for n, at in enumerate(SENDS):
        copy_bytes(packed.at[at, 0 : STRIPS - 1], a2a_send.at[n]).wait()


def turned(result, out_s, out_r):
    for q, (f, t) in enumerate(PHASES):
        out = out_s if f == 1 else out_r
        for b in range(OUTX // SUB):
            block = result[q, b].T
            out[t, :, SUB * b : SUB * (b + 1)] = jnp.concatenate([block[0:ROWS], block[ROWS:]], axis=1)


def local(image_grad, source_field, receiver_field):
    vmem = pltpu.VMEM
    dma = pltpu.SemaphoreType.DMA
    result = pl.pallas_call(
        kernel,
        out_shape=jax.ShapeDtypeStruct((4, OUTX // SUB, HALF, 128), F32),
        in_specs=[pl.BlockSpec(memory_space=pltpu.HBM)] * 3,
        out_specs=pl.BlockSpec(memory_space=pltpu.VMEM),
        scratch_shapes=[
            vmem((2, NK, 8, NX), F32),
            vmem((NK * XB, SLOT, 128), F32),
            vmem((NK * XB, ROWS, 128), F32),
            vmem((PAIRS, NX + 16, 128), F32),
            vmem((PAIRS * NX + 2 * PADF, 128), F32),
            vmem((4, STRIPS, PIECE, 128), F32),
            vmem((4, COLS, STRIPS * ROWS), F32),
            vmem((4, STRIPS * PIECE, 128), F32),
            vmem((NX + 2 * PADD, 128), F32),
            vmem((2, NX + 2 * PADX, 128), F32),
            vmem((2, XB, NK, 128), F32),
            vmem((2, XB, NK, 128), F32),
            vmem((SUBX, 128), F32),
            vmem((4, 3, 2, HALF, 128), F32),
            vmem((4, 2, HALF, 128), F32),
            vmem((4, 2, 2, HALF, 128), F32),
            vmem((4, 2, HALF, 128), F32),
            dma,
            dma((4,)),
            dma((CHUNKS,)),
            dma((3,)),
            dma((3,)),
            dma((2,)),
            dma((2,)),
            dma((24,)),
            dma((24,)),
        ],
        compiler_params=pltpu.CompilerParams(
            collective_id=0, has_side_effects=True, vmem_limit_bytes=VMEM
        ),
        name="adjoint",
    )(image_grad, jnp.swapaxes(source_field, 1, 2), jnp.swapaxes(receiver_field, 1, 2))
    out = jax.ShapeDtypeStruct((2, ROWS, OUTX), F32)
    return pl.pallas_call(
        turned,
        out_shape=(out, out),
        in_specs=[pl.BlockSpec(memory_space=pltpu.VMEM)],
        out_specs=[pl.BlockSpec(memory_space=pltpu.VMEM)] * 2,
        compiler_params=pltpu.CompilerParams(vmem_limit_bytes=4 << 20),
        name="turned",
    )(result)


def solution(mesh):
    in_specs = (P("lag", "strip", None), P(None, None, "strip"), P(None, None, "strip"))
    out_specs = (P(None, "strip", "lag"), P(None, "strip", "lag"))
    return jax.shard_map(local, mesh=mesh, in_specs=in_specs, out_specs=out_specs, check_vma=False)
```
